32 devices in a mesh: seq: 4 (over x, core), expert: 8 (over z, y).
Axes of the slice: x: 2, y: 2, z: 4, core: 2. Of those that a mesh axis runs over, the one named last changes fastest.
Arguments:
- tokens: bfloat16 [8, 896, 2048], P('expert', 'seq'), may hold values from -96 to 96
- slot_keys: bfloat16 [2048, 64], P(None, 'expert'), may hold values from -2 to 2
- w_in: bfloat16 [8, 2048, 6144], P('expert', None, 'seq'), may hold values from -0.125 to 0.125
- w_out: bfloat16 [8, 6144, 2048], P('expert', 'seq'), may hold values from -0.078125 to 0.078125
Outputs:
- mixed: bfloat16 [8, 896, 2048], P('expert', 'seq')
The draws below stay inside these ranges and needn't reach their ends.
All inputs are finite; a program needn't handle non-finite values.
Results may differ from the reference program's by a relative error of at most 0.012.
Values may be sent and summed in bfloat16 or wider, within the bound.
No kernel may reach another device: no remote copies, remote signals or barrier semaphores. Data moves between devices by JAX's collectives and lax.ppermute only.
A program may use at most 64 MiB of HBM per device.

```python
import math
import jax
import jax.numpy as jnp
from jax import lax

D = 2048
FFN = 6144
SLOT_EXP = 8
EXPERTS = 8
SLOTS = 64
SEQS = 8
LEN = 896


def key_table(key):
    raw_table = jax.random.normal(jax.random.fold_in(key, 11), (D, SLOTS), jnp.float32) * (3.0 / math.sqrt(D))
    return jnp.clip(raw_table, -2.0, 2.0)


def draw_slot_keys(key, part):
    return key_table(key).astype(jnp.bfloat16)


def draw_tokens(key, part):
    base_key = jax.random.fold_in(key, 23)
    values = jax.random.normal(base_key, (SEQS, LEN, D), jnp.float32)
    return jnp.clip(values, -96.0, 96.0).astype(jnp.bfloat16)


def levels(stream_key, shape, cuts, low, largest):
    def one(dim, shards_of):
        steps = jax.random.uniform(jax.random.fold_in(jax.random.fold_in(stream_key, 6), dim), (shards_of,), jnp.float32, low / len(cuts), largest / len(cuts))
        return jnp.repeat(jnp.exp(steps), shape[dim] // shards_of).reshape((-1,) + (1,) * (len(shape) - dim - 1))

    factor_of = one(*cuts[0])
    for cut in cuts[1:]:
        factor_of = factor_of * one(*cut)
    return factor_of


def scatter_about(rng, shape, spread, limit, shards=(), kind=jnp.bfloat16):
    values = jax.random.normal(rng, shape, jnp.float32) * spread
    if len(shards) > 0:
        values = levels(rng, shape, shards, -0.22, 0.18) * values
    return jnp.clip(values, min=-limit, max=limit).astype(kind)


def setup_inputs(seed: int = 0) -> dict:
    arg_keys = jax.random.split(jax.random.key(seed), 5)
    return {
        "tokens": draw_tokens(jax.random.fold_in(arg_keys[4], 71), 0),
        "slot_keys": draw_slot_keys(jax.random.fold_in(arg_keys[4], 71), 0),
        "w_in": scatter_about(arg_keys[2], (EXPERTS, D, FFN), D ** -0.5, 0.125, ((0, 8), (2, 4))),
        "w_out": scatter_about(arg_keys[3], (EXPERTS, FFN, D), FFN ** -0.5, 0.078125, ((0, 8), (1, 4))),
    }


def dispatch(seq_tokens, slot_keys):
    logits = jnp.dot(seq_tokens, slot_keys, preferred_element_type=jnp.float32)
    top_score = jnp.max(logits, axis=0)
    weights = jnp.exp(logits - top_score[None, :]).astype(jnp.bfloat16)
    totals = jnp.sum(weights.astype(jnp.float32), axis=0)
    summed = jnp.dot(weights.T, seq_tokens, preferred_element_type=jnp.float32)
    return (summed / totals[:, None]).astype(jnp.bfloat16)


def run_expert(packed):
    expert_rows, matrix_in, matrix_out = packed
    hidden = jax.nn.gelu(jnp.dot(expert_rows, matrix_in, preferred_element_type=jnp.float32), approximate=True).astype(jnp.bfloat16)
    return jnp.dot(hidden, matrix_out, preferred_element_type=jnp.float32).astype(jnp.bfloat16)


def reference(tokens, slot_keys, w_in, w_out):
    slot_inputs = lax.map(lambda seq_tokens: dispatch(seq_tokens, slot_keys), tokens)
    by_expert = slot_inputs.reshape(SEQS, EXPERTS, SLOT_EXP, D).transpose(1, 0, 2, 3).reshape(EXPERTS, SEQS * SLOT_EXP, D)
    expert_out = lax.map(run_expert, (by_expert, w_in, w_out))
    slot_outputs = expert_out.reshape(EXPERTS, SEQS, SLOT_EXP, D).transpose(1, 0, 2, 3).reshape(SEQS, SLOTS, D)

    def combine(packed):
        seq_tokens, outputs = packed
        logits = jnp.dot(seq_tokens, slot_keys, preferred_element_type=jnp.float32)
        row_top = jnp.max(logits, axis=1)
        raised = jnp.exp(logits - row_top[:, None])
        mix_weights = (raised / jnp.sum(raised, axis=1)[:, None]).astype(jnp.bfloat16)
        return jnp.dot(mix_weights, outputs, preferred_element_type=jnp.float32).astype(jnp.bfloat16)

    return lax.map(combine, (tokens, slot_outputs))
```

```python
import functools

import jax
import jax.numpy as jnp
from jax import lax
from jax.experimental import pallas as pl
from jax.experimental.pallas import tpu as pltpu
from jax.sharding import Mesh, PartitionSpec as P

F32 = jnp.float32
BF16 = jnp.bfloat16
LANES = 128
SWAP = ((0, 1), (1, 0))


def column_halves(half):
    core = lax.axis_index("core")
    own = pl.ds(pl.multiple_of(core * half, LANES), half)
    other = pl.ds(pl.multiple_of((1 - core) * half, LANES), half)
    return own, other


def three_terms(value):
    first = value.astype(BF16).astype(F32)
    rest = value - first
    second = rest.astype(BF16).astype(F32)
    return first, second, rest - second


def stats_tile(top, total):
    shape = top.shape[:-1] + (LANES,)
    lane = lax.broadcasted_iota(jnp.int32, shape, len(shape) - 1)
    tile = jnp.zeros(shape, F32)
    for place, term in enumerate(three_terms(top) + three_terms(total)):
        tile = jnp.where(lane == place, term, tile)
    return tile


def read_stats(tile):
    top = tile[..., 0:1] + tile[..., 1:2] + tile[..., 2:3]
    total = tile[..., 3:4] + tile[..., 4:5] + tile[..., 5:6]
    return top, total


def dispatch_kernel(got_ref, swapped_ref, tok_ref, keep_ref, stats_ref, send_ref, mix_ref):
    half = got_ref.shape[2]
    slots = keep_ref.shape[0]
    own, other = column_halves(half)
    rows_by_cols = (((1,), (1,)), ((), ()))
    logits = lax.dot_general(
        got_ref[...].reshape(slots, half), tok_ref[:, own], rows_by_cols, preferred_element_type=F32
    ) + lax.dot_general(
        swapped_ref[...].reshape(slots, half), tok_ref[:, other], rows_by_cols, preferred_element_type=F32
    )
    top = jnp.max(logits, axis=1, keepdims=True)
    weights = jnp.exp(logits - top).astype(BF16)
    total = jnp.sum(weights.astype(F32), axis=1, keepdims=True)
    send_ref[:, :half] = jnp.dot(weights, tok_ref[:, other], preferred_element_type=F32).astype(BF16)
    send_ref[:, half:] = stats_tile(top, total).astype(BF16)
    keep_ref[...] = jnp.dot(weights, tok_ref[:, own], preferred_element_type=F32)
    lane = lax.broadcasted_iota(jnp.int32, stats_ref.shape, 1)
    stats_ref[...] = jnp.where(lane == 0, top, total)
    raised = jnp.exp(logits - jnp.max(logits, axis=0, keepdims=True))
    mix_ref[...] = (raised / jnp.sum(raised, axis=0, keepdims=True)).astype(BF16)


def chip_sum_kernel(keep_ref, stats_ref, came_ref, out_ref):
    half = keep_ref.shape[1]
    experts, chips, rows, _ = out_ref.shape
    top, total = stats_ref[:, 0:1], stats_ref[:, 1:2]
    came_top, came_total = read_stats(came_ref[:, half:].astype(F32))
    new_top = jnp.maximum(top, came_top)
    scale, came_scale = jnp.exp(top - new_top), jnp.exp(came_top - new_top)
    sums = (keep_ref[...] * scale + came_ref[:, :half].astype(F32) * came_scale).astype(BF16)
    tile = stats_tile(new_top, total * scale + came_total * came_scale).astype(BF16)
    sums = sums.reshape(experts, rows, half)
    tile = tile.reshape(experts, rows, LANES)
    for chip in range(chips):
        out_ref[:, chip, :, :half] = sums
        out_ref[:, chip, :, half:] = tile


def slot_inputs_of(ref):
    seqs, chips, rows, width = ref.shape
    half = width - LANES
    stats = [read_stats(ref[:, chip, :, half:].astype(F32)) for chip in range(chips)]
    top = functools.reduce(jnp.maximum, [s[0] for s in stats])
    scales = [jnp.exp(s[0] - top) for s in stats]
    total = sum(scale * s[1] for scale, s in zip(scales, stats))
    summed = sum(ref[:, chip, :, :half].astype(F32) * scales[chip] for chip in range(chips))
    return (summed / total).reshape(seqs * rows, half).astype(BF16)


def expert_kernel(
    chunks, mine_ref, swapped_ref, w_in_ref, w_out_ref, keep_ref, send_ref,
    w_in_buf, w_out_buf, acc_in, acc_out, hidden, sem_in, sem_out,
):
    width, units = w_in_buf.shape
    half = width // 2
    core = lax.axis_index("core")
    own, other = column_halves(half)
    step_in, step_out = width // chunks, units // chunks
    half_chunks = chunks // 2

    def row_start(k):
        side = core if k < half_chunks else 1 - core
        return pl.multiple_of(side * half + (k % half_chunks) * step_in, LANES)

    copies_in, copies_out = [], []
    for k in range(chunks):
        rows = pl.ds(row_start(k), step_in)
        copies_in.append(pltpu.make_async_copy(w_in_ref.at[rows], w_in_buf.at[rows], sem_in.at[k]))
        copies_in[-1].start()
    for k in range(chunks):
        rows = pl.ds(k * step_out, step_out)
        copies_out.append(pltpu.make_async_copy(w_out_ref.at[rows], w_out_buf.at[rows], sem_out.at[k]))
        copies_out[-1].start()
    sides = (slot_inputs_of(mine_ref), slot_inputs_of(swapped_ref))
    for k in range(chunks):
        copies_in[k].wait()
        start = (k % half_chunks) * step_in
        term = jnp.dot(
            sides[k // half_chunks][:, start : start + step_in],
            w_in_buf[pl.ds(row_start(k), step_in), :],
            preferred_element_type=F32,
        )
        acc_in[...] = term if k == 0 else acc_in[...] + term
    hidden[...] = jax.nn.gelu(acc_in[...], approximate=True).astype(BF16)
    for k in range(chunks):
        copies_out[k].wait()
        rows = pl.ds(k * step_out, step_out)
        left = hidden[:, k * step_out : (k + 1) * step_out]
        sent = jnp.dot(left, w_out_buf[rows, other], preferred_element_type=F32)
        acc_out[...] = sent if k == 0 else acc_out[...] + sent
        kept = jnp.dot(left, w_out_buf[rows, own], preferred_element_type=F32)
        keep_ref[...] = kept if k == 0 else keep_ref[...] + kept
    send_ref[...] = acc_out[...].astype(BF16)


def pair_sum_kernel(keep_ref, came_ref, out_ref):
    seqs, chips, rows, half = out_ref.shape
    sums = (keep_ref[...] + came_ref[...].astype(F32)).astype(BF16).reshape(seqs, rows, half)
    for chip in range(chips):
        out_ref[:, chip] = sums


def mix_kernel(mix_ref, mine_ref, swapped_ref, out_ref):
    experts, chips, rows, half = mine_ref.shape
    for cols, ref in zip(column_halves(half), (mine_ref, swapped_ref)):
        summed = sum(ref[:, chip].astype(F32) for chip in range(chips))
        slot_outputs = summed.reshape(experts * rows, half).astype(BF16)
        out_ref[:, cols] = lax.dot_general(
            mix_ref[...], slot_outputs, (((0,), (0,)), ((), ())), preferred_element_type=F32
        ).astype(BF16)


def call(kernel, outs, *args, scratch=(), in_hbm=(), flops=0, limit=16 << 20):
    size = sum(a.size * a.dtype.itemsize for a in args)
    specs = [
        pl.BlockSpec(memory_space=pltpu.HBM if i in in_hbm else pltpu.VMEM) for i in range(len(args))
    ]
    return pl.pallas_call(
        kernel,
        out_shape=[jax.ShapeDtypeStruct(shape, dtype) for shape, dtype in outs],
        in_specs=specs,
        out_specs=[pl.BlockSpec(memory_space=pltpu.VMEM)] * len(outs),
        scratch_shapes=list(scratch),
        compiler_params=pltpu.CompilerParams(vmem_limit_bytes=limit),
        cost_estimate=pl.CostEstimate(flops=flops, bytes_accessed=size, transcendentals=0),
    )(*args)


def on_device(tokens, slot_keys, w_in, w_out):
    token_rows = tokens[0]
    count, width = token_rows.shape
    half = width // 2
    per_expert = slot_keys.shape[1]
    experts, chips = lax.axis_size("expert"), lax.axis_size("chip")
    slots = experts * per_expert
    units = w_in.shape[2]

    keys = lax.dynamic_slice_in_dim(slot_keys.T, lax.axis_index("core") * half, half, 1)
    keys = jnp.broadcast_to(keys[None], (experts, per_expert, half))
    got = lax.all_to_all(keys, "expert", split_axis=0, concat_axis=0, tiled=True)
    swapped = lax.ppermute(got, "core", SWAP)
    keep, stats, send, mix = call(
        dispatch_kernel,
        [
            ((slots, half), F32),
            ((slots, LANES), F32),
            ((slots, half + LANES), BF16),
            ((slots, count), BF16),
        ],
        got, swapped, token_rows,
        flops=4 * slots * count * width,
    )
    came = lax.ppermute(send, "core", SWAP)
    (packed,) = call(
        chip_sum_kernel,
        [((experts, chips, per_expert, half + LANES), BF16)],
        keep, stats, came,
    )
    both = ("expert", "chip")
    flat = packed.reshape((experts * chips,) + packed.shape[2:])
    mine = lax.all_to_all(flat, both, split_axis=0, concat_axis=0, tiled=True)
    swapped = lax.ppermute(mine, "core", SWAP)
    chunks = 4
    keep, send = call(
        functools.partial(expert_kernel, chunks),
        [((slots, half), F32), ((slots, half), BF16)],
        mine.reshape(packed.shape), swapped.reshape(packed.shape), w_in[0], w_out[0],
        scratch=[
            pltpu.VMEM((width, units), BF16),
            pltpu.VMEM((units, width), BF16),
            pltpu.VMEM((slots, units), F32),
            pltpu.VMEM((slots, half), F32),
            pltpu.VMEM((slots, units), BF16),
            pltpu.SemaphoreType.DMA((chunks,)),
            pltpu.SemaphoreType.DMA((chunks,)),
        ],
        in_hbm=(2, 3),
        flops=4 * slots * width * units,
        limit=40 << 20,
    )
    came = lax.ppermute(send, "core", SWAP)
    (packed,) = call(pair_sum_kernel, [((experts, chips, per_expert, half), BF16)], keep, came)
    flat = packed.reshape((experts * chips,) + packed.shape[2:])
    mine = lax.all_to_all(flat, both, split_axis=0, concat_axis=0, tiled=True)
    swapped = lax.ppermute(mine, "core", SWAP)
    (mixed,) = call(
        mix_kernel,
        [((count, width), BF16)],
        mix, mine.reshape(packed.shape), swapped.reshape(packed.shape),
        flops=2 * slots * count * width,
    )
    return mixed[None]


def solution(mesh):
    sizes, names = [], []
    for name in mesh.axis_names:
        if name == "seq":
            sizes += [mesh.shape[name] // 2, 2]
            names += ["chip", "core"]
        else:
            sizes.append(mesh.shape[name])
            names.append(name)
    split = Mesh(mesh.devices.reshape(sizes), tuple(names))
    seq = ("chip", "core")
    placed = (
        P("expert", seq, None),
        P(None, "expert"),
        P("expert", None, seq),
        P("expert", seq, None),
    )
    return jax.shard_map(
        on_device, mesh=split, in_specs=placed, out_specs=P("expert", seq, None), check_vma=False
    )
```

```python
import functools

import jax
import jax.numpy as jnp
from jax import lax
from jax.experimental import pallas as pl
from jax.experimental.pallas import tpu as pltpu
from jax.sharding import Mesh, PartitionSpec as P

F32 = jnp.float32
BF16 = jnp.bfloat16
LANES = 128
SWAP = ((0, 1), (1, 0))


def column_halves(half):
    core = lax.axis_index("core")
    own = pl.ds(pl.multiple_of(core * half, LANES), half)
    other = pl.ds(pl.multiple_of((1 - core) * half, LANES), half)
    return own, other


def three_terms(value):
    first = value.astype(BF16).astype(F32)
    rest = value - first
    second = rest.astype(BF16).astype(F32)
    return first, second, rest - second


def stats_tile(top, total):
    shape = top.shape[:-1] + (LANES,)
    lane = lax.broadcasted_iota(jnp.int32, shape, len(shape) - 1)
    tile = jnp.zeros(shape, F32)
    for place, term in enumerate(three_terms(top) + three_terms(total)):
        tile = jnp.where(lane == place, term, tile)
    return tile


def read_stats(tile):
    top = tile[..., 0:1] + tile[..., 1:2] + tile[..., 2:3]
    total = tile[..., 3:4] + tile[..., 4:5] + tile[..., 5:6]
    return top, total


def dispatch_kernel(got_ref, swapped_ref, tok_ref, keep_ref, stats_ref, send_ref, mix_ref):
    half = got_ref.shape[2]
    slots = keep_ref.shape[0]
    own, other = column_halves(half)
    rows_by_cols = (((1,), (1,)), ((), ()))
    logits = lax.dot_general(
        got_ref[...].reshape(slots, half), tok_ref[:, own], rows_by_cols, preferred_element_type=F32
    ) + lax.dot_general(
        swapped_ref[...].reshape(slots, half), tok_ref[:, other], rows_by_cols, preferred_element_type=F32
    )
    top = jnp.max(logits, axis=1, keepdims=True)
    weights = jnp.exp(logits - top).astype(BF16)
    total = jnp.sum(weights.astype(F32), axis=1, keepdims=True)
    send_ref[:, :half] = jnp.dot(weights, tok_ref[:, other], preferred_element_type=F32).astype(BF16)
    send_ref[:, half:] = stats_tile(top, total).astype(BF16)
    keep_ref[...] = jnp.dot(weights, tok_ref[:, own], preferred_element_type=F32)
    lane = lax.broadcasted_iota(jnp.int32, stats_ref.shape, 1)
    stats_ref[...] = jnp.where(lane == 0, top, total)
    raised = jnp.exp(logits - jnp.max(logits, axis=0, keepdims=True))
    mix_ref[...] = (raised / jnp.sum(raised, axis=0, keepdims=True)).astype(BF16)


def chip_sum_kernel(keep_ref, stats_ref, came_ref, out_ref):
    half = keep_ref.shape[1]
    experts, chips, rows, _ = out_ref.shape
    top, total = stats_ref[:, 0:1], stats_ref[:, 1:2]
    came_top, came_total = read_stats(came_ref[:, half:].astype(F32))
    new_top = jnp.maximum(top, came_top)
    scale, came_scale = jnp.exp(top - new_top), jnp.exp(came_top - new_top)
    sums = (keep_ref[...] * scale + came_ref[:, :half].astype(F32) * came_scale).astype(BF16)
    tile = stats_tile(new_top, total * scale + came_total * came_scale).astype(BF16)
    sums = sums.reshape(experts, rows, half)
    tile = tile.reshape(experts, rows, LANES)
    for chip in range(chips):
        out_ref[:, chip, :, :half] = sums
        out_ref[:, chip, :, half:] = tile


def slot_inputs_of(ref):
    seqs, chips, rows, width = ref.shape
    half = width - LANES
    stats = [read_stats(ref[:, chip, :, half:].astype(F32)) for chip in range(chips)]
    top = functools.reduce(jnp.maximum, [s[0] for s in stats])
    scales = [jnp.exp(s[0] - top) for s in stats]
    total = sum(scale * s[1] for scale, s in zip(scales, stats))
    summed = sum(ref[:, chip, :, :half].astype(F32) * scales[chip] for chip in range(chips))
    return (summed / total).reshape(seqs * rows, half).astype(BF16)


def fetch_kernel(sides, *refs):
    count = len(sides)
    core = lax.axis_index("core")
    copies = []
    for i, side in enumerate(sides):
        rows = refs[count + i].shape[0]
        block = {"own": core, "other": 1 - core, "first": 0}[side]
        source = refs[i].at[pl.ds(pl.multiple_of(block * rows, LANES // 4), rows)]
        copies.append(pltpu.make_async_copy(source, refs[count + i], refs[2 * count].at[i]))
    for copy in copies:
        copy.start()
    for copy in copies:
        copy.wait()


def expert_kernel(
    mine_ref, swapped_ref, w_own_ref, w_other_ref, w_first_ref, w_out_ref, keep_ref, send_ref,
    w_second, sem,
):
    half = w_own_ref.shape[0]
    rows = w_first_ref.shape[0]
    own, other = column_halves(half)
    copy = pltpu.make_async_copy(w_out_ref.at[pl.ds(rows, rows)], w_second, sem)
    copy.start()
    summed = jnp.dot(
        slot_inputs_of(mine_ref), w_own_ref[...], preferred_element_type=F32
    ) + jnp.dot(slot_inputs_of(swapped_ref), w_other_ref[...], preferred_element_type=F32)
    hidden = jax.nn.gelu(summed, approximate=True).astype(BF16)
    first, second = hidden[:, :rows], hidden[:, rows:]
    sent = jnp.dot(first, w_first_ref[:, other], preferred_element_type=F32)
    kept = jnp.dot(first, w_first_ref[:, own], preferred_element_type=F32)
    copy.wait()
    sent += jnp.dot(second, w_second[:, other], preferred_element_type=F32)
    send_ref[...] = sent.astype(BF16)
    keep_ref[...] = kept + jnp.dot(second, w_second[:, own], preferred_element_type=F32)


def pair_sum_kernel(keep_ref, came_ref, out_ref):
    seqs, chips, rows, half = out_ref.shape
    sums = (keep_ref[...] + came_ref[...].astype(F32)).astype(BF16).reshape(seqs, rows, half)
    for chip in range(chips):
        out_ref[:, chip] = sums


def mix_kernel(mix_ref, mine_ref, swapped_ref, out_ref):
    experts, chips, rows, half = mine_ref.shape
    for cols, ref in zip(column_halves(half), (mine_ref, swapped_ref)):
        summed = sum(ref[:, chip].astype(F32) for chip in range(chips))
        slot_outputs = summed.reshape(experts * rows, half).astype(BF16)
        out_ref[:, cols] = lax.dot_general(
            mix_ref[...], slot_outputs, (((0,), (0,)), ((), ())), preferred_element_type=F32
        ).astype(BF16)


def nbytes(arrays):
    return sum(a.size * a.dtype.itemsize for a in arrays)


def call(kernel, outs, *args, scratch=(), in_hbm=(), stay=False, flops=0, limit=16 << 20):
    return pl.pallas_call(
        kernel,
        out_shape=[
            (pltpu.VMEM if stay else jax.ShapeDtypeStruct)(shape, dtype) for shape, dtype in outs
        ],
        in_specs=[
            pl.BlockSpec(memory_space=pltpu.HBM if i in in_hbm else pltpu.VMEM)
            for i in range(len(args))
        ],
        out_specs=[pl.BlockSpec(memory_space=pltpu.VMEM)] * len(outs),
        scratch_shapes=list(scratch),
        compiler_params=pltpu.CompilerParams(vmem_limit_bytes=limit),
        cost_estimate=pl.CostEstimate(flops=flops, bytes_accessed=nbytes(args), transcendentals=0),
    )(*args)


def fetch(after, *parts):
    after, *arrays = lax.optimization_barrier((after,) + tuple(a for a, _, _ in parts))
    outs = [((rows,) + a.shape[1:], a.dtype) for a, _, rows in parts]
    near = call(
        functools.partial(fetch_kernel, [side for _, side, _ in parts]),
        outs,
        *[pltpu.with_memory_space_constraint(a, pltpu.HBM) for a in arrays],
        scratch=[pltpu.SemaphoreType.DMA((len(parts),))],
        in_hbm=range(len(parts)),
        stay=True,
        limit=4 << 20,
    )
    return after, near


def on_device(tokens, slot_keys, w_in, w_out):
    token_rows = tokens[0]
    count, width = token_rows.shape
    half = width // 2
    per_expert = slot_keys.shape[1]
    experts, chips = lax.axis_size("expert"), lax.axis_size("chip")
    slots = experts * per_expert
    units = w_in.shape[2]

    keys = lax.dynamic_slice_in_dim(slot_keys.T, lax.axis_index("core") * half, half, 1)
    keys = jnp.broadcast_to(keys[None], (experts, per_expert, half))
    got = lax.all_to_all(keys, "expert", split_axis=0, concat_axis=0, tiled=True)
    got, (near_rows, w_own) = fetch(
        got, (token_rows, "first", count), (w_in[0], "own", half)
    )
    swapped = lax.ppermute(got, "core", SWAP)
    swapped, near_rows, w_own = lax.optimization_barrier((swapped, near_rows, w_own))
    keep, stats, send, mix = call(
        dispatch_kernel,
        [
            ((slots, half), F32),
            ((slots, LANES), F32),
            ((slots, half + LANES), BF16),
            ((slots, count), BF16),
        ],
        got, swapped, near_rows,
        flops=4 * slots * count * width,
    )
    send, (w_other,) = fetch(send, (w_in[0], "other", half))
    came = lax.ppermute(send, "core", SWAP)
    came, w_other = lax.optimization_barrier((came, w_other))
    (packed,) = call(
        chip_sum_kernel,
        [((experts, chips, per_expert, half + LANES), BF16)],
        keep, stats, came,
    )
    both = ("expert", "chip")
    flat = packed.reshape((experts * chips,) + packed.shape[2:])
    mine = lax.all_to_all(flat, both, split_axis=0, concat_axis=0, tiled=True)
    mine, (w_first,) = fetch(mine, (w_out[0], "first", units // 2))
    swapped = lax.ppermute(mine, "core", SWAP)
    swapped, w_first = lax.optimization_barrier((swapped, w_first))
    held = (w_own, w_other, w_first)
    keep, send = call(
        expert_kernel,
        [((slots, half), F32), ((slots, half), BF16)],
        mine.reshape(packed.shape), swapped.reshape(packed.shape), *held,
        pltpu.with_memory_space_constraint(w_out[0], pltpu.HBM),
        scratch=[pltpu.VMEM((units // 2, width), BF16), pltpu.SemaphoreType.DMA],
        in_hbm=(5,),
        flops=4 * slots * width * units,
        limit=24 << 20,
    )
    came = lax.ppermute(send, "core", SWAP)
    (packed,) = call(pair_sum_kernel, [((experts, chips, per_expert, half), BF16)], keep, came)
    flat = packed.reshape((experts * chips,) + packed.shape[2:])
    mine = lax.all_to_all(flat, both, split_axis=0, concat_axis=0, tiled=True)
    swapped = lax.ppermute(mine, "core", SWAP)
    (mixed,) = call(
        mix_kernel,
        [((count, width), BF16)],
        mix, mine.reshape(packed.shape), swapped.reshape(packed.shape),
        flops=2 * slots * count * width,
    )
    return mixed[None]


def solution(mesh):
    sizes, names = [], []
    for name in mesh.axis_names:
        if name == "seq":
            sizes += [mesh.shape[name] // 2, 2]
            names += ["chip", "core"]
        else:
            sizes.append(mesh.shape[name])
            names.append(name)
    split = Mesh(mesh.devices.reshape(sizes), tuple(names))
    seq = ("chip", "core")
    placed = (
        P("expert", seq, None),
        P(None, "expert"),
        P("expert", None, seq),
        P("expert", seq, None),
    )
    return jax.shard_map(
        on_device, mesh=split, in_specs=placed, out_specs=P("expert", seq, None), check_vma=False
    )
```

```python
import functools
import math

import jax
import jax.numpy as jnp
from jax import lax
from jax.experimental import pallas as pl
from jax.experimental.pallas import tpu as pltpu
from jax.sharding import Mesh, PartitionSpec as P

F32 = jnp.float32
BF16 = jnp.bfloat16
LANES = 128
SWAP = ((0, 1), (1, 0))
ROWS_BY_ROWS = (((1,), (1,)), ((), ()))


def column_halves(half):
    core = lax.axis_index("core")
    own = pl.ds(pl.multiple_of(core * half, LANES), half)
    other = pl.ds(pl.multiple_of((1 - core) * half, LANES), half)
    return own, other


def three_terms(value):
    first = value.astype(BF16).astype(F32)
    rest = value - first
    second = rest.astype(BF16).astype(F32)
    return first, second, rest - second


def stats_tile(top, total):
    shape = top.shape[:-1] + (LANES,)
    lane = lax.broadcasted_iota(jnp.int32, shape, len(shape) - 1)
    tile = jnp.zeros(shape, F32)
    for place, term in enumerate(three_terms(top) + three_terms(total)):
        tile = jnp.where(lane == place, term, tile)
    return tile


def read_stats(tile):
    top = tile[..., 0:1] + tile[..., 1:2] + tile[..., 2:3]
    total = tile[..., 3:4] + tile[..., 4:5] + tile[..., 5:6]
    return top, total


def copy_parts(sem, pairs):
    copies = [pltpu.make_async_copy(src, dst, sem.at[i]) for i, (src, dst) in enumerate(pairs)]
    for copy in copies:
        copy.start()
    return copies


def block_rows(start, count):
    return pl.ds(pl.multiple_of(start, LANES), count)


def first_fetch_kernel(tok_ref, w_in_ref, near_tok, near_w, sem):
    half = w_in_ref.shape[0] // 2
    rows = near_w.shape[0]
    start = lax.axis_index("core") * half
    pairs = [(tok_ref, near_tok), (w_in_ref.at[block_rows(start, rows)], near_w)]
    for copy in copy_parts(sem, pairs):
        copy.wait()


def own_logits_kernel(got_ref, tok_ref, w_in_ref, part_ref, near_w, sem):
    slots = part_ref.shape[0]
    half = got_ref.shape[2]
    rows = near_w.shape[0]
    start = lax.axis_index("core") * half + (half - rows)
    copies = copy_parts(sem, [(w_in_ref.at[block_rows(start, rows)], near_w)])
    own, _ = column_halves(half)
    part_ref[...] = lax.dot_general(
        got_ref[...].reshape(slots, half), tok_ref[:, own], ROWS_BY_ROWS, preferred_element_type=F32
    )
    for copy in copies:
        copy.wait()


def send_sums_kernel(swapped_ref, part_ref, tok_ref, logits_ref, weights_ref, stats_ref, send_ref):
    half = swapped_ref.shape[2]
    slots = part_ref.shape[0]
    _, other = column_halves(half)
    logits = part_ref[...] + lax.dot_general(
        swapped_ref[...].reshape(slots, half), tok_ref[:, other], ROWS_BY_ROWS,
        preferred_element_type=F32,
    )
    logits_ref[...] = logits
    top = jnp.max(logits, axis=1, keepdims=True)
    weights = jnp.exp(logits - top).astype(BF16)
    weights_ref[...] = weights
    total = jnp.sum(weights.astype(F32), axis=1, keepdims=True)
    send_ref[:, :half] = jnp.dot(weights, tok_ref[:, other], preferred_element_type=F32).astype(BF16)
    send_ref[:, half:] = stats_tile(top, total).astype(BF16)
    lane = lax.broadcasted_iota(jnp.int32, stats_ref.shape, 1)
    stats_ref[...] = jnp.where(lane == 0, top, total)


def keep_sums_kernel(logits_ref, weights_ref, tok_ref, w_in_ref, keep_ref, mix_ref, near_w, sem):
    half = keep_ref.shape[1]
    start = (1 - lax.axis_index("core")) * half
    copies = copy_parts(sem, [(w_in_ref.at[block_rows(start, near_w.shape[0])], near_w)])
    own, _ = column_halves(half)
    keep_ref[...] = jnp.dot(weights_ref[...], tok_ref[:, own], preferred_element_type=F32)
    logits = logits_ref[...]
    raised = jnp.exp(logits - jnp.max(logits, axis=0, keepdims=True))
    mix_ref[...] = (raised / jnp.sum(raised, axis=0, keepdims=True)).astype(BF16)
    for copy in copies:
        copy.wait()


def chip_sum_kernel(keep_ref, stats_ref, came_ref, out_ref):
    half = keep_ref.shape[1]
    experts, chips, rows, _ = out_ref.shape
    top, total = stats_ref[:, 0:1], stats_ref[:, 1:2]
    came_top, came_total = read_stats(came_ref[:, half:].astype(F32))
    new_top = jnp.maximum(top, came_top)
    scale, came_scale = jnp.exp(top - new_top), jnp.exp(came_top - new_top)
    sums = (keep_ref[...] * scale + came_ref[:, :half].astype(F32) * came_scale).astype(BF16)
    tile = stats_tile(new_top, total * scale + came_total * came_scale).astype(BF16)
    sums = sums.reshape(experts, rows, half)
    tile = tile.reshape(experts, rows, LANES)
    for chip in range(chips):
        out_ref[:, chip, :, :half] = sums
        out_ref[:, chip, :, half:] = tile


def slot_inputs_of(ref):
    seqs, chips, rows, width = ref.shape
    half = width - LANES
    stats = [read_stats(ref[:, chip, :, half:].astype(F32)) for chip in range(chips)]
    top = functools.reduce(jnp.maximum, [s[0] for s in stats])
    scales = [jnp.exp(s[0] - top) for s in stats]
    total = sum(scale * s[1] for scale, s in zip(scales, stats))
    summed = sum(ref[:, chip, :, :half].astype(F32) * scales[chip] for chip in range(chips))
    return (summed / total).reshape(seqs * rows, half).astype(BF16)


def row_blocks_dot(left, blocks):
    start, total = 0, 0
    for block in blocks:
        rows = block.shape[0]
        total += jnp.dot(left[:, start : start + rows], block[...], preferred_element_type=F32)
        start += rows
    return total


def own_hidden_kernel(
    mine_ref, w_first_ref, w_second_ref, w_in_ref, w_out_ref, acc_ref, near_in, near_out, sem
):
    half = w_in_ref.shape[0] // 2
    rows = near_in.shape[0]
    start = (1 - lax.axis_index("core")) * half + (half - rows)
    _, other = column_halves(half)
    copies = copy_parts(sem, [
        (w_in_ref.at[block_rows(start, rows)], near_in),
        (w_out_ref.at[pl.ds(0, near_out.shape[0]), other], near_out),
    ])
    acc_ref[...] = row_blocks_dot(slot_inputs_of(mine_ref), (w_first_ref, w_second_ref))
    for copy in copies:
        copy.wait()


def send_terms_kernel(
    acc_ref, swapped_ref, w_first_ref, w_second_ref, w_sent_ref, w_out_ref,
    send_ref, hidden_ref, near_kept, rest, sem,
):
    own, other = column_halves(w_out_ref.shape[1] // 2)
    start = w_sent_ref.shape[0]
    copies = copy_parts(sem, [
        (w_out_ref.at[pl.ds(start, rest.shape[0]), other], rest),
        (w_out_ref.at[pl.ds(0, near_kept.shape[0]), own], near_kept),
    ])
    summed = acc_ref[...] + row_blocks_dot(slot_inputs_of(swapped_ref), (w_first_ref, w_second_ref))
    hidden = jax.nn.gelu(summed, approximate=True).astype(BF16)
    hidden_ref[...] = hidden
    sent = jnp.dot(hidden[:, :start], w_sent_ref[...], preferred_element_type=F32)
    copies[0].wait()
    sent += jnp.dot(hidden[:, start:], rest[...], preferred_element_type=F32)
    send_ref[...] = sent.astype(BF16)
    copies[1].wait()


def keep_terms_kernel(hidden_ref, w_kept_ref, w_out_ref, keep_ref, rest, sem):
    own, _ = column_halves(w_out_ref.shape[1] // 2)
    start = w_kept_ref.shape[0]
    copies = copy_parts(sem, [(w_out_ref.at[pl.ds(start, rest.shape[0]), own], rest)])
    kept = jnp.dot(hidden_ref[:, :start], w_kept_ref[...], preferred_element_type=F32)
    copies[0].wait()
    keep_ref[...] = kept + jnp.dot(hidden_ref[:, start:], rest[...], preferred_element_type=F32)


def pair_sum_kernel(keep_ref, came_ref, out_ref):
    seqs, chips, rows, half = out_ref.shape
    sums = (keep_ref[...] + came_ref[...].astype(F32)).astype(BF16).reshape(seqs, rows, half)
    for chip in range(chips):
        out_ref[:, chip] = sums


def mixed_half(mix_ref, ref):
    experts, chips, rows, half = ref.shape
    summed = sum(ref[:, chip].astype(F32) for chip in range(chips))
    slot_outputs = summed.reshape(experts * rows, half).astype(BF16)
    return lax.dot_general(
        mix_ref[...], slot_outputs, (((0,), (0,)), ((), ())), preferred_element_type=F32
    ).astype(BF16)


def own_mix_kernel(mix_ref, mine_ref, half_ref):
    half_ref[...] = mixed_half(mix_ref, mine_ref)


def mix_kernel(mix_ref, swapped_ref, half_ref, out_ref, rest, sem):
    own, other = column_halves(half_ref.shape[1])
    copies = copy_parts(sem, [(half_ref, out_ref.at[:, own])])
    rest[...] = mixed_half(mix_ref, swapped_ref)
    last = pltpu.make_async_copy(rest, out_ref.at[:, other], sem.at[1])
    last.start()
    copies[0].wait()
    last.wait()


def call(kernel, outs, *args, scratch=(), copies=0, in_hbm=(), stay=(), flops=0, limit=8 << 20):
    if copies:
        scratch = tuple(scratch) + (pltpu.SemaphoreType.DMA((copies,)),)
    shapes, out_specs = [], []
    for i, (shape, dtype) in enumerate(outs):
        shapes.append((pltpu.VMEM if i in stay else jax.ShapeDtypeStruct)(shape, dtype))
        out_specs.append(pl.BlockSpec(memory_space=pltpu.VMEM))
    return pl.pallas_call(
        kernel,
        out_shape=shapes,
        in_specs=[
            pl.BlockSpec(memory_space=pltpu.HBM if i in in_hbm else pltpu.VMEM)
            for i in range(len(args))
        ],
        out_specs=out_specs,
        scratch_shapes=list(scratch),
        compiler_params=pltpu.CompilerParams(vmem_limit_bytes=limit),
        cost_estimate=pl.CostEstimate(
            flops=flops,
            bytes_accessed=sum(math.prod(shape) * jnp.dtype(dtype).itemsize for shape, dtype in outs),
            transcendentals=0,
        ),
    )(*[
        pltpu.with_memory_space_constraint(a, pltpu.HBM) if i in in_hbm else a
        for i, a in enumerate(args)
    ])


def share(count, numerator, denominator):
    return max(LANES, count * numerator // denominator // LANES * LANES)


def on_device(tokens, slot_keys, w_in, w_out):
    token_rows, w_in, w_out = tokens[0], w_in[0], w_out[0]
    count, width = token_rows.shape
    half = width // 2
    per_expert = slot_keys.shape[1]
    experts, chips = lax.axis_size("expert"), lax.axis_size("chip")
    slots = experts * per_expert
    units = w_in.shape[1]
    own_rows, other_rows = share(half, 5, 8), share(half, 1, 2)
    sent_rows, kept_rows = share(units, 1, 4), share(units, 1, 3)

    keys = lax.dynamic_slice_in_dim(slot_keys.T, lax.axis_index("core") * half, half, 1)
    keys = jnp.broadcast_to(keys[None], (experts, per_expert, half))
    got = lax.all_to_all(keys, "expert", split_axis=0, concat_axis=0, tiled=True)
    near_tok, w_own_first = call(
        first_fetch_kernel,
        [(token_rows.shape, BF16), ((own_rows, units), BF16)],
        token_rows, w_in,
        copies=2, in_hbm=(0, 1), stay=(0, 1),
    )
    got, near_tok, w_own_first = lax.optimization_barrier((got, near_tok, w_own_first))
    swapped = lax.ppermute(got, "core", SWAP)
    part, w_own_second = call(
        own_logits_kernel,
        [((slots, count), F32), ((half - own_rows, units), BF16)],
        got, near_tok, w_in,
        copies=1, in_hbm=(2,), stay=(1,), flops=2 * slots * count * half,
    )
    logits, weights, stats, send = call(
        send_sums_kernel,
        [
            ((slots, count), F32),
            ((slots, count), BF16),
            ((slots, LANES), F32),
            ((slots, half + LANES), BF16),
        ],
        swapped, part, near_tok,
        flops=4 * slots * count * half,
    )
    came = lax.ppermute(send, "core", SWAP)
    keep, mix, w_other_first = call(
        keep_sums_kernel,
        [((slots, half), F32), ((slots, count), BF16), ((other_rows, units), BF16)],
        logits, weights, near_tok, w_in,
        copies=1, in_hbm=(3,), stay=(2,), flops=2 * slots * count * half,
    )
    (packed,) = call(
        chip_sum_kernel,
        [((experts, chips, per_expert, half + LANES), BF16)],
        keep, stats, came,
        limit=16 << 20,
    )
    both = ("expert", "chip")
    flat = packed.reshape((experts * chips,) + packed.shape[2:])
    mine = lax.all_to_all(flat, both, split_axis=0, concat_axis=0, tiled=True)
    swapped = lax.ppermute(mine, "core", SWAP)
    acc, w_other_second, w_sent = call(
        own_hidden_kernel,
        [((slots, units), F32), ((half - other_rows, units), BF16), ((sent_rows, half), BF16)],
        mine.reshape(packed.shape), w_own_first, w_own_second, w_in, w_out,
        copies=2, in_hbm=(3, 4), stay=(1, 2), flops=2 * slots * half * units, limit=16 << 20,
    )
    send, hidden, w_kept = call(
        send_terms_kernel,
        [((slots, half), BF16), ((slots, units), BF16), ((kept_rows, half), BF16)],
        acc, swapped.reshape(packed.shape), w_other_first, w_other_second, w_sent, w_out,
        scratch=[pltpu.VMEM((units - sent_rows, half), BF16)],
        copies=2, in_hbm=(5,), stay=(2,), flops=4 * slots * half * units, limit=16 << 20,
    )
    came = lax.ppermute(send, "core", SWAP)
    (keep,) = call(
        keep_terms_kernel,
        [((slots, half), F32)],
        hidden, w_kept, w_out,
        scratch=[pltpu.VMEM((units - kept_rows, half), BF16)],
        copies=1, in_hbm=(2,), flops=2 * slots * half * units,
    )
    (packed,) = call(
        pair_sum_kernel, [((experts, chips, per_expert, half), BF16)], keep, came, limit=16 << 20
    )
    flat = packed.reshape((experts * chips,) + packed.shape[2:])
    mine = lax.all_to_all(flat, both, split_axis=0, concat_axis=0, tiled=True)
    swapped = lax.ppermute(mine, "core", SWAP)
    (own_half,) = call(
        own_mix_kernel,
        [((count, half), BF16)],
        mix, mine.reshape(packed.shape),
        stay=(0,), flops=2 * slots * count * half, limit=16 << 20,
    )
    mixed = pl.pallas_call(
        mix_kernel,
        out_shape=jax.ShapeDtypeStruct((count, width), BF16),
        in_specs=[pl.BlockSpec(memory_space=pltpu.VMEM)] * 3,
        out_specs=pl.BlockSpec(memory_space=pltpu.HBM),
        scratch_shapes=[pltpu.VMEM((count, half), BF16), pltpu.SemaphoreType.DMA((2,))],
        compiler_params=pltpu.CompilerParams(vmem_limit_bytes=16 << 20),
        cost_estimate=pl.CostEstimate(
            flops=2 * slots * count * half, bytes_accessed=2 * count * width, transcendentals=0
        ),
    )(mix, swapped.reshape(packed.shape), own_half)
    return mixed[None]


def solution(mesh):
    sizes, names = [], []
    for name in mesh.axis_names:
        if name == "seq":
            sizes += [mesh.shape[name] // 2, 2]
            names += ["chip", "core"]
        else:
            sizes.append(mesh.shape[name])
            names.append(name)
    split = Mesh(mesh.devices.reshape(sizes), tuple(names))
    seq = ("chip", "core")
    placed = (
        P("expert", seq, None),
        P(None, "expert"),
        P("expert", None, seq),
        P("expert", seq, None),
    )
    return jax.shard_map(
        on_device, mesh=split, in_specs=placed, out_specs=P("expert", seq, None), check_vma=False
    )
```

```python
import functools
import math

import jax
import jax.numpy as jnp
from jax import lax
from jax.experimental import pallas as pl
from jax.experimental.pallas import tpu as pltpu
from jax.sharding import Mesh, PartitionSpec as P

F32 = jnp.float32
BF16 = jnp.bfloat16
LANES = 128
SWAP = ((0, 1), (1, 0))
ROWS_BY_ROWS = (((1,), (1,)), ((), ()))


def column_halves(half):
    core = lax.axis_index("core")
    own = pl.ds(pl.multiple_of(core * half, LANES), half)
    other = pl.ds(pl.multiple_of((1 - core) * half, LANES), half)
    return own, other


def three_terms(value):
    first = value.astype(BF16).astype(F32)
    rest = value - first
    second = rest.astype(BF16).astype(F32)
    return first, second, rest - second


def stats_tile(top, total):
    shape = top.shape[:-1] + (LANES,)
    lane = lax.broadcasted_iota(jnp.int32, shape, len(shape) - 1)
    tile = jnp.zeros(shape, F32)
    for place, term in enumerate(three_terms(top) + three_terms(total)):
        tile = jnp.where(lane == place, term, tile)
    return tile


def read_stats(tile):
    top = tile[..., 0:1] + tile[..., 1:2] + tile[..., 2:3]
    total = tile[..., 3:4] + tile[..., 4:5] + tile[..., 5:6]
    return top, total


def copy_parts(sem, pairs):
    copies = [pltpu.make_async_copy(src, dst, sem.at[i]) for i, (src, dst) in enumerate(pairs)]
    for copy in copies:
        copy.start()
    return copies


def block_rows(start, count):
    return pl.ds(pl.multiple_of(start, LANES), count)


def first_fetch_kernel(tok_ref, w_in_ref, near_tok, near_w, sem):
    half = w_in_ref.shape[0] // 2
    rows = near_w.shape[0]
    start = lax.axis_index("core") * half
    pairs = [(tok_ref, near_tok), (w_in_ref.at[block_rows(start, rows)], near_w)]
    for copy in copy_parts(sem, pairs):
        copy.wait()


def own_logits_kernel(got_ref, tok_ref, w_in_ref, part_ref, near_own, near_other, sem):
    slots = part_ref.shape[0]
    half = got_ref.shape[2]
    core = lax.axis_index("core")
    rows = near_own.shape[0]
    copies = copy_parts(sem, [
        (w_in_ref.at[block_rows(core * half + (half - rows), rows)], near_own),
        (w_in_ref.at[block_rows((1 - core) * half, near_other.shape[0])], near_other),
    ])
    own, _ = column_halves(half)
    part_ref[...] = lax.dot_general(
        got_ref[...].reshape(slots, half), tok_ref[:, own], ROWS_BY_ROWS, preferred_element_type=F32
    )
    for copy in copies:
        copy.wait()


def send_sums_kernel(swapped_ref, part_ref, tok_ref, logits_ref, weights_ref, stats_ref, send_ref):
    half = swapped_ref.shape[2]
    slots = part_ref.shape[0]
    _, other = column_halves(half)
    logits = part_ref[...] + lax.dot_general(
        swapped_ref[...].reshape(slots, half), tok_ref[:, other], ROWS_BY_ROWS,
        preferred_element_type=F32,
    )
    logits_ref[...] = logits
    top = jnp.max(logits, axis=1, keepdims=True)
    weights = jnp.exp(logits - top).astype(BF16)
    weights_ref[...] = weights
    total = jnp.sum(weights.astype(F32), axis=1, keepdims=True)
    send_ref[:, :half] = jnp.dot(weights, tok_ref[:, other], preferred_element_type=F32).astype(BF16)
    send_ref[:, half:] = stats_tile(top, total).astype(BF16)
    lane = lax.broadcasted_iota(jnp.int32, stats_ref.shape, 1)
    stats_ref[...] = jnp.where(lane == 0, top, total)


def keep_sums_kernel(
    skip, logits_ref, weights_ref, tok_ref, w_in_ref, keep_ref, mix_ref, near_w, sem
):
    half = keep_ref.shape[1]
    start = (1 - lax.axis_index("core")) * half + skip
    copies = copy_parts(sem, [(w_in_ref.at[block_rows(start, near_w.shape[0])], near_w)])
    own, _ = column_halves(half)
    keep_ref[...] = jnp.dot(weights_ref[...], tok_ref[:, own], preferred_element_type=F32)
    logits = logits_ref[...]
    raised = jnp.exp(logits - jnp.max(logits, axis=0, keepdims=True))
    mix_ref[...] = (raised / jnp.sum(raised, axis=0, keepdims=True)).astype(BF16)
    for copy in copies:
        copy.wait()


def chip_sum_kernel(keep_ref, stats_ref, came_ref, out_ref):
    half = keep_ref.shape[1]
    experts, chips, rows, _ = out_ref.shape
    top, total = stats_ref[:, 0:1], stats_ref[:, 1:2]
    came_top, came_total = read_stats(came_ref[:, half:].astype(F32))
    new_top = jnp.maximum(top, came_top)
    scale, came_scale = jnp.exp(top - new_top), jnp.exp(came_top - new_top)
    sums = (keep_ref[...] * scale + came_ref[:, :half].astype(F32) * came_scale).astype(BF16)
    tile = stats_tile(new_top, total * scale + came_total * came_scale).astype(BF16)
    sums = sums.reshape(experts, rows, half)
    tile = tile.reshape(experts, rows, LANES)
    for chip in range(chips):
        out_ref[:, chip, :, :half] = sums
        out_ref[:, chip, :, half:] = tile


def slot_inputs_of(ref):
    seqs, chips, rows, width = ref.shape
    half = width - LANES
    stats = [read_stats(ref[:, chip, :, half:].astype(F32)) for chip in range(chips)]
    top = functools.reduce(jnp.maximum, [s[0] for s in stats])
    scales = [jnp.exp(s[0] - top) for s in stats]
    total = sum(scale * s[1] for scale, s in zip(scales, stats))
    summed = sum(ref[:, chip, :, :half].astype(F32) * scales[chip] for chip in range(chips))
    return (summed / total).reshape(seqs * rows, half).astype(BF16)


def row_blocks_dot(left, blocks):
    start, total = 0, 0
    for block in blocks:
        rows = block.shape[0]
        total += jnp.dot(left[:, start : start + rows], block[...], preferred_element_type=F32)
        start += rows
    return total


def own_hidden_kernel(
    mine_ref, w_first_ref, w_second_ref, w_in_ref, w_out_ref, acc_ref, near_in, near_out, sem
):
    half = w_in_ref.shape[0] // 2
    rows = near_in.shape[0]
    start = (1 - lax.axis_index("core")) * half + (half - rows)
    copies = copy_parts(sem, [
        (w_in_ref.at[block_rows(start, rows)], near_in),
        (w_out_ref.at[pl.ds(0, near_out.shape[0])], near_out),
    ])
    acc_ref[...] = row_blocks_dot(slot_inputs_of(mine_ref), (w_first_ref, w_second_ref))
    for copy in copies:
        copy.wait()


def send_terms_kernel(
    acc_ref, swapped_ref, w_first_ref, w_second_ref, w_third_ref, w_near_ref, w_out_ref,
    send_ref, hidden_ref, rest, sem,
):
    _, other = column_halves(w_out_ref.shape[1] // 2)
    near, pieces = w_near_ref.shape[0], sem.shape[0]
    step = rest.shape[0] // pieces
    copies = copy_parts(sem, [
        (w_out_ref.at[pl.ds(near + i * step, step)], rest.at[pl.ds(i * step, step)])
        for i in range(pieces)
    ])
    summed = acc_ref[...] + row_blocks_dot(
        slot_inputs_of(swapped_ref), (w_first_ref, w_second_ref, w_third_ref)
    )
    hidden = jax.nn.gelu(summed, approximate=True).astype(BF16)
    hidden_ref[...] = hidden
    sent = jnp.dot(hidden[:, :near], w_near_ref[:, other], preferred_element_type=F32)
    for i, copy in enumerate(copies):
        copy.wait()
        rows = pl.ds(near + i * step, step)
        sent += jnp.dot(
            hidden_ref[:, rows], rest[pl.ds(i * step, step), other], preferred_element_type=F32
        )
    send_ref[...] = sent.astype(BF16)


def keep_terms_kernel(hidden_ref, w_near_ref, w_rest_ref, keep_ref):
    own, _ = column_halves(keep_ref.shape[1])
    near = w_near_ref.shape[0]
    keep_ref[...] = jnp.dot(
        hidden_ref[:, :near], w_near_ref[:, own], preferred_element_type=F32
    ) + jnp.dot(hidden_ref[:, near:], w_rest_ref[:, own], preferred_element_type=F32)


def pair_sum_kernel(keep_ref, came_ref, out_ref):
    seqs, chips, rows, half = out_ref.shape
    sums = (keep_ref[...] + came_ref[...].astype(F32)).astype(BF16).reshape(seqs, rows, half)
    for chip in range(chips):
        out_ref[:, chip] = sums


def mixed_half(mix_ref, ref):
    experts, chips, rows, half = ref.shape
    summed = sum(ref[:, chip].astype(F32) for chip in range(chips))
    slot_outputs = summed.reshape(experts * rows, half).astype(BF16)
    return lax.dot_general(
        mix_ref[...], slot_outputs, (((0,), (0,)), ((), ())), preferred_element_type=F32
    ).astype(BF16)


def own_mix_kernel(mix_ref, mine_ref, half_ref):
    half_ref[...] = mixed_half(mix_ref, mine_ref)


def mix_kernel(mix_ref, swapped_ref, half_ref, out_ref, rest, sem):
    own, other = column_halves(half_ref.shape[1])
    copies = copy_parts(sem, [(half_ref, out_ref.at[:, own])])
    rest[...] = mixed_half(mix_ref, swapped_ref)
    last = pltpu.make_async_copy(rest, out_ref.at[:, other], sem.at[1])
    last.start()
    copies[0].wait()
    last.wait()


def call(kernel, outs, *args, scratch=(), copies=0, in_hbm=(), stay=(), flops=0, limit=8 << 20):
    if copies:
        scratch = tuple(scratch) + (pltpu.SemaphoreType.DMA((copies,)),)
    shapes, out_specs = [], []
    for i, (shape, dtype) in enumerate(outs):
        shapes.append((pltpu.VMEM if i in stay else jax.ShapeDtypeStruct)(shape, dtype))
        out_specs.append(pl.BlockSpec(memory_space=pltpu.VMEM))
    return pl.pallas_call(
        kernel,
        out_shape=shapes,
        in_specs=[
            pl.BlockSpec(memory_space=pltpu.HBM if i in in_hbm else pltpu.VMEM)
            for i in range(len(args))
        ],
        out_specs=out_specs,
        scratch_shapes=list(scratch),
        compiler_params=pltpu.CompilerParams(vmem_limit_bytes=limit),
        cost_estimate=pl.CostEstimate(
            flops=flops,
            bytes_accessed=sum(math.prod(shape) * jnp.dtype(dtype).itemsize for shape, dtype in outs),
            transcendentals=0,
        ),
    )(*[
        pltpu.with_memory_space_constraint(a, pltpu.HBM) if i in in_hbm else a
        for i, a in enumerate(args)
    ])


def share(count, numerator, denominator):
    return max(LANES, count * numerator // denominator // LANES * LANES)


def on_device(tokens, slot_keys, w_in, w_out):
    token_rows, w_in, w_out = tokens[0], w_in[0], w_out[0]
    count, width = token_rows.shape
    half = width // 2
    per_expert = slot_keys.shape[1]
    experts, chips = lax.axis_size("expert"), lax.axis_size("chip")
    slots = experts * per_expert
    units = w_in.shape[1]
    own_rows = share(half, 3, 4)
    other_rows = (share(half, 1, 4), share(half, 1, 2), half - share(half, 1, 4) - share(half, 1, 2))
    near_units = share(units, 1, 6)

    keys = lax.dynamic_slice_in_dim(slot_keys.T, lax.axis_index("core") * half, half, 1)
    keys = jnp.broadcast_to(keys[None], (experts, per_expert, half))
    got = lax.all_to_all(keys, "expert", split_axis=0, concat_axis=0, tiled=True)
    near_tok, w_own_first = call(
        first_fetch_kernel,
        [(token_rows.shape, BF16), ((own_rows, units), BF16)],
        token_rows, w_in,
        copies=2, in_hbm=(0, 1), stay=(0, 1),
    )
    got, near_tok, w_own_first = lax.optimization_barrier((got, near_tok, w_own_first))
    swapped = lax.ppermute(got, "core", SWAP)
    part, w_own_second, w_other_first = call(
        own_logits_kernel,
        [
            ((slots, count), F32),
            ((half - own_rows, units), BF16),
            ((other_rows[0], units), BF16),
        ],
        got, near_tok, w_in,
        copies=2, in_hbm=(2,), stay=(1, 2), flops=2 * slots * count * half,
    )
    logits, weights, stats, send = call(
        send_sums_kernel,
        [
            ((slots, count), F32),
            ((slots, count), BF16),
            ((slots, LANES), F32),
            ((slots, half + LANES), BF16),
        ],
        swapped, part, near_tok,
        flops=4 * slots * count * half,
    )
    came = lax.ppermute(send, "core", SWAP)
    keep, mix, w_other_second = call(
        functools.partial(keep_sums_kernel, other_rows[0]),
        [((slots, half), F32), ((slots, count), BF16), ((other_rows[1], units), BF16)],
        logits, weights, near_tok, w_in,
        copies=1, in_hbm=(3,), stay=(2,), flops=2 * slots * count * half,
    )
    (packed,) = call(
        chip_sum_kernel,
        [((experts, chips, per_expert, half + LANES), BF16)],
        keep, stats, came,
        limit=16 << 20,
    )
    both = ("expert", "chip")
    flat = packed.reshape((experts * chips,) + packed.shape[2:])
    mine = lax.all_to_all(flat, both, split_axis=0, concat_axis=0, tiled=True)
    swapped = lax.ppermute(mine, "core", SWAP)
    acc, w_other_third, w_near = call(
        own_hidden_kernel,
        [((slots, units), F32), ((other_rows[2], units), BF16), ((near_units, width), BF16)],
        mine.reshape(packed.shape), w_own_first, w_own_second, w_in, w_out,
        copies=2, in_hbm=(3, 4), stay=(1, 2), flops=2 * slots * half * units, limit=16 << 20,
    )
    w_other = (w_other_first, w_other_second, w_other_third)
    pieces = math.gcd((units - near_units) // LANES, 5)
    send, hidden, w_rest = call(
        send_terms_kernel,
        [((slots, half), BF16), ((slots, units), BF16), ((units - near_units, width), BF16)],
        acc, swapped.reshape(packed.shape), *w_other, w_near, w_out,
        copies=pieces, in_hbm=(6,), stay=(2,), flops=4 * slots * half * units, limit=16 << 20,
    )
    came = lax.ppermute(send, "core", SWAP)
    (keep,) = call(
        keep_terms_kernel,
        [((slots, half), F32)],
        hidden, w_near, w_rest,
        flops=2 * slots * half * units,
    )
    (packed,) = call(
        pair_sum_kernel, [((experts, chips, per_expert, half), BF16)], keep, came, limit=16 << 20
    )
    flat = packed.reshape((experts * chips,) + packed.shape[2:])
    mine = lax.all_to_all(flat, both, split_axis=0, concat_axis=0, tiled=True)
    swapped = lax.ppermute(mine, "core", SWAP)
    (own_half,) = call(
        own_mix_kernel,
        [((count, half), BF16)],
        mix, mine.reshape(packed.shape),
        stay=(0,), flops=2 * slots * count * half, limit=16 << 20,
    )
    mixed = pl.pallas_call(
        mix_kernel,
        out_shape=jax.ShapeDtypeStruct((count, width), BF16),
        in_specs=[pl.BlockSpec(memory_space=pltpu.VMEM)] * 3,
        out_specs=pl.BlockSpec(memory_space=pltpu.HBM),
        scratch_shapes=[pltpu.VMEM((count, half), BF16), pltpu.SemaphoreType.DMA((2,))],
        compiler_params=pltpu.CompilerParams(vmem_limit_bytes=16 << 20),
        cost_estimate=pl.CostEstimate(
            flops=2 * slots * count * half, bytes_accessed=2 * count * width, transcendentals=0
        ),
    )(mix, swapped.reshape(packed.shape), own_half)
    return mixed[None]


def solution(mesh):
    sizes, names = [], []
    for name in mesh.axis_names:
        if name == "seq":
            sizes += [mesh.shape[name] // 2, 2]
            names += ["chip", "core"]
        else:
            sizes.append(mesh.shape[name])
            names.append(name)
    split = Mesh(mesh.devices.reshape(sizes), tuple(names))
    seq = ("chip", "core")
    placed = (
        P("expert", seq, None),
        P(None, "expert"),
        P("expert", None, seq),
        P("expert", seq, None),
    )
    return jax.shard_map(
        on_device, mesh=split, in_specs=placed, out_specs=P("expert", seq, None), check_vma=False
    )
```

```python
import functools
import math

import jax
import jax.numpy as jnp
from jax import lax
from jax.experimental import pallas as pl
from jax.experimental.pallas import tpu as pltpu
from jax.sharding import Mesh, PartitionSpec as P

F32 = jnp.float32
BF16 = jnp.bfloat16
LANES = 128
SWAP = ((0, 1), (1, 0))
ROWS_BY_ROWS = (((1,), (1,)), ((), ()))


def column_halves(half):
    core = lax.axis_index("core")
    own = pl.ds(pl.multiple_of(core * half, LANES), half)
    other = pl.ds(pl.multiple_of((1 - core) * half, LANES), half)
    return own, other


def three_terms(value):
    first = value.astype(BF16).astype(F32)
    rest = value - first
    second = rest.astype(BF16).astype(F32)
    return first, second, rest - second


def stats_tile(top, total):
    shape = top.shape[:-1] + (LANES,)
    lane = lax.broadcasted_iota(jnp.int32, shape, len(shape) - 1)
    tile = jnp.zeros(shape, F32)
    for place, term in enumerate(three_terms(top) + three_terms(total)):
        tile = jnp.where(lane == place, term, tile)
    return tile


def read_stats(tile):
    top = tile[..., 0:1] + tile[..., 1:2] + tile[..., 2:3]
    total = tile[..., 3:4] + tile[..., 4:5] + tile[..., 5:6]
    return top, total


def copy_parts(sem, pairs):
    copies = [pltpu.make_async_copy(src, dst, sem.at[i]) for i, (src, dst) in enumerate(pairs)]
    for copy in copies:
        copy.start()
    return copies


def block_rows(start, count):
    return pl.ds(pl.multiple_of(start, LANES), count)


def held_masks(experts):
    return [((2 + 2 * k) % experts, experts - 1 - 2 * k) for k in range(experts // 2)]


def gather_keys(keys, experts, chips):
    axes = ("chip", "core", "expert")
    blocks = []
    for masks in held_masks(experts):
        pairs = [
            (((chip * 2 + core) * experts + e), ((chip * 2 + core) * experts + (e ^ mask)))
            for chip in range(chips)
            for core, mask in enumerate(masks)
            if mask
            for e in range(experts)
        ]
        blocks.append(lax.ppermute(keys, axes, pairs))
    return blocks


def stack_kernel(*refs):
    keys_ref, *blocks, out_ref = refs
    for k, block in enumerate(blocks[:-1]):
        out_ref[k] = block[...]
    out_ref[len(blocks) - 1] = jnp.where(
        lax.axis_index("core") == 0, keys_ref[...], blocks[-1][...]
    )


def first_fetch_kernel(tok_ref, w_in_ref, near_tok, near_w, sem):
    rows = near_w.shape[0]
    start = lax.axis_index("core") * rows
    pairs = [(tok_ref, near_tok), (w_in_ref.at[block_rows(start, rows)], near_w)]
    for copy in copy_parts(sem, pairs):
        copy.wait()


def held_logits(stack_ref, tok_ref):
    blocks, rows, width = stack_ref.shape
    return lax.dot_general(
        stack_ref[...].reshape(blocks * rows, width), tok_ref[...], ROWS_BY_ROWS,
        preferred_element_type=F32,
    )


def held_logits_kernel(stack_ref, tok_ref, w_in_ref, part_ref, near_w, sem):
    start = (1 - lax.axis_index("core")) * (w_in_ref.shape[0] // 2)
    copies = copy_parts(sem, [(w_in_ref.at[block_rows(start, near_w.shape[0])], near_w)])
    part_ref[...] = held_logits(stack_ref, tok_ref)
    for copy in copies:
        copy.wait()


def send_sums_kernel(
    swapped_ref, part_ref, tok_ref, logits_ref, weights_ref, stats_ref, send_ref, sorted_ref
):
    half = tok_ref.shape[1] // 2
    _, other = column_halves(half)
    experts, rows, count = sorted_ref.shape
    expert, core = lax.axis_index("expert"), lax.axis_index("core")
    theirs = held_logits(swapped_ref, tok_ref)
    for k, (even, odd) in enumerate(held_masks(experts)):
        held = slice(k * rows, (k + 1) * rows)
        sorted_ref[expert ^ jnp.where(core == 0, even, odd)] = part_ref[held, :]
        sorted_ref[expert ^ jnp.where(core == 0, odd, even)] = theirs[held, :]
    logits = sorted_ref[...].reshape(experts * rows, count)
    logits_ref[...] = logits
    top = jnp.max(logits, axis=1, keepdims=True)
    weights = jnp.exp(logits - top).astype(BF16)
    weights_ref[...] = weights
    total = jnp.sum(weights.astype(F32), axis=1, keepdims=True)
    send_ref[:, :half] = jnp.dot(weights, tok_ref[:, other], preferred_element_type=F32).astype(BF16)
    send_ref[:, half:] = stats_tile(top, total).astype(BF16)
    lane = lax.broadcasted_iota(jnp.int32, stats_ref.shape, 1)
    stats_ref[...] = jnp.where(lane == 0, top, total)


def keep_sums_kernel(
    skip, logits_ref, weights_ref, tok_ref, w_in_ref, keep_ref, mix_ref, near_w, sem
):
    half = keep_ref.shape[1]
    start = (1 - lax.axis_index("core")) * half + skip
    copies = copy_parts(sem, [(w_in_ref.at[block_rows(start, near_w.shape[0])], near_w)])
    own, _ = column_halves(half)
    keep_ref[...] = jnp.dot(weights_ref[...], tok_ref[:, own], preferred_element_type=F32)
    logits = logits_ref[...]
    raised = jnp.exp(logits - jnp.max(logits, axis=0, keepdims=True))
    mix_ref[...] = (raised / jnp.sum(raised, axis=0, keepdims=True)).astype(BF16)
    for copy in copies:
        copy.wait()


def chip_sum_kernel(keep_ref, stats_ref, came_ref, out_ref):
    half = keep_ref.shape[1]
    experts, chips, rows, _ = out_ref.shape
    top, total = stats_ref[:, 0:1], stats_ref[:, 1:2]
    came_top, came_total = read_stats(came_ref[:, half:].astype(F32))
    new_top = jnp.maximum(top, came_top)
    scale, came_scale = jnp.exp(top - new_top), jnp.exp(came_top - new_top)
    sums = (keep_ref[...] * scale + came_ref[:, :half].astype(F32) * came_scale).astype(BF16)
    tile = stats_tile(new_top, total * scale + came_total * came_scale).astype(BF16)
    sums = sums.reshape(experts, rows, half)
    tile = tile.reshape(experts, rows, LANES)
    for chip in range(chips):
        out_ref[:, chip, :, :half] = sums
        out_ref[:, chip, :, half:] = tile


def slot_inputs_of(ref):
    seqs, chips, rows, width = ref.shape
    half = width - LANES
    stats = [read_stats(ref[:, chip, :, half:].astype(F32)) for chip in range(chips)]
    top = functools.reduce(jnp.maximum, [s[0] for s in stats])
    scales = [jnp.exp(s[0] - top) for s in stats]
    total = sum(scale * s[1] for scale, s in zip(scales, stats))
    summed = sum(ref[:, chip, :, :half].astype(F32) * scales[chip] for chip in range(chips))
    return (summed / total).reshape(seqs * rows, half).astype(BF16)


def row_blocks_dot(left, blocks):
    start, total = 0, 0
    for block in blocks:
        rows = block.shape[0]
        total += jnp.dot(left[:, start : start + rows], block[...], preferred_element_type=F32)
        start += rows
    return total


def own_hidden_kernel(
    mine_ref, w_own_ref, w_out_ref, acc_ref, near_out, sem
):
    copies = copy_parts(sem, [(w_out_ref.at[pl.ds(0, near_out.shape[0])], near_out)])
    acc_ref[...] = row_blocks_dot(slot_inputs_of(mine_ref), (w_own_ref,))
    for copy in copies:
        copy.wait()


def send_terms_kernel(
    acc_ref, swapped_ref, w_first_ref, w_second_ref, w_near_ref, w_out_ref,
    send_ref, hidden_ref, rest, sem,
):
    _, other = column_halves(w_out_ref.shape[1] // 2)
    near, pieces = w_near_ref.shape[0], sem.shape[0]
    step = rest.shape[0] // pieces
    copies = copy_parts(sem, [
        (w_out_ref.at[pl.ds(near + i * step, step)], rest.at[pl.ds(i * step, step)])
        for i in range(pieces)
    ])
    summed = acc_ref[...] + row_blocks_dot(slot_inputs_of(swapped_ref), (w_first_ref, w_second_ref))
    hidden = jax.nn.gelu(summed, approximate=True).astype(BF16)
    hidden_ref[...] = hidden
    sent = jnp.dot(hidden[:, :near], w_near_ref[:, other], preferred_element_type=F32)
    for i, copy in enumerate(copies):
        copy.wait()
        rows = pl.ds(near + i * step, step)
        sent += jnp.dot(
            hidden_ref[:, rows], rest[pl.ds(i * step, step), other], preferred_element_type=F32
        )
    send_ref[...] = sent.astype(BF16)


def keep_terms_kernel(hidden_ref, w_near_ref, w_rest_ref, keep_ref):
    own, _ = column_halves(keep_ref.shape[1])
    near = w_near_ref.shape[0]
    keep_ref[...] = jnp.dot(
        hidden_ref[:, :near], w_near_ref[:, own], preferred_element_type=F32
    ) + jnp.dot(hidden_ref[:, near:], w_rest_ref[:, own], preferred_element_type=F32)


def pair_sum_kernel(keep_ref, came_ref, out_ref):
    seqs, chips, rows, half = out_ref.shape
    sums = (keep_ref[...] + came_ref[...].astype(F32)).astype(BF16).reshape(seqs, rows, half)
    for chip in range(chips):
        out_ref[:, chip] = sums


def mixed_half(mix_ref, ref):
    experts, chips, rows, half = ref.shape
    summed = sum(ref[:, chip].astype(F32) for chip in range(chips))
    slot_outputs = summed.reshape(experts * rows, half).astype(BF16)
    return lax.dot_general(
        mix_ref[...], slot_outputs, (((0,), (0,)), ((), ())), preferred_element_type=F32
    ).astype(BF16)


def own_mix_kernel(mix_ref, mine_ref, half_ref):
    half_ref[...] = mixed_half(mix_ref, mine_ref)


def mix_kernel(mix_ref, swapped_ref, half_ref, out_ref, rest, sem):
    own, other = column_halves(half_ref.shape[1])
    copies = copy_parts(sem, [(half_ref, out_ref.at[:, own])])
    rest[...] = mixed_half(mix_ref, swapped_ref)
    last = pltpu.make_async_copy(rest, out_ref.at[:, other], sem.at[1])
    last.start()
    copies[0].wait()
    last.wait()


def call(kernel, outs, *args, scratch=(), copies=0, in_hbm=(), stay=(), flops=0, limit=8 << 20):
    if copies:
        scratch = tuple(scratch) + (pltpu.SemaphoreType.DMA((copies,)),)
    shapes, out_specs = [], []
    for i, (shape, dtype) in enumerate(outs):
        shapes.append((pltpu.VMEM if i in stay else jax.ShapeDtypeStruct)(shape, dtype))
        out_specs.append(pl.BlockSpec(memory_space=pltpu.VMEM))
    return pl.pallas_call(
        kernel,
        out_shape=shapes,
        in_specs=[
            pl.BlockSpec(memory_space=pltpu.HBM if i in in_hbm else pltpu.VMEM)
            for i in range(len(args))
        ],
        out_specs=out_specs,
        scratch_shapes=list(scratch),
        compiler_params=pltpu.CompilerParams(vmem_limit_bytes=limit),
        cost_estimate=pl.CostEstimate(
            flops=flops,
            bytes_accessed=sum(math.prod(shape) * jnp.dtype(dtype).itemsize for shape, dtype in outs),
            transcendentals=0,
        ),
    )(*[
        pltpu.with_memory_space_constraint(a, pltpu.HBM) if i in in_hbm else a
        for i, a in enumerate(args)
    ])


def share(count, numerator, denominator):
    return max(LANES, count * numerator // denominator // LANES * LANES)


def on_device(tokens, slot_keys, w_in, w_out):
    token_rows, w_in, w_out = tokens[0], w_in[0], w_out[0]
    count, width = token_rows.shape
    half = width // 2
    per_expert = slot_keys.shape[1]
    experts, chips = lax.axis_size("expert"), lax.axis_size("chip")
    slots = experts * per_expert
    units = w_in.shape[1]
    other_rows = share(half, 1, 2)
    near_units = share(units, 1, 3)

    keys = slot_keys.T
    blocks = gather_keys(keys, experts, chips)
    near_tok, w_own = call(
        first_fetch_kernel,
        [(token_rows.shape, BF16), ((half, units), BF16)],
        token_rows, w_in,
        copies=2, in_hbm=(0, 1), stay=(0, 1),
    )
    *blocks, near_tok, w_own = lax.optimization_barrier((*blocks, near_tok, w_own))
    (stack,) = call(
        stack_kernel, [((experts // 2, per_expert, width), BF16)], keys, *blocks
    )
    swapped = lax.ppermute(stack, "core", SWAP)
    part, w_other_first = call(
        held_logits_kernel,
        [((slots // 2, count), F32), ((other_rows, units), BF16)],
        stack, near_tok, w_in,
        copies=1, in_hbm=(2,), stay=(1,), flops=2 * slots * count * half,
    )
    logits, weights, stats, send = call(
        send_sums_kernel,
        [
            ((slots, count), F32),
            ((slots, count), BF16),
            ((slots, LANES), F32),
            ((slots, half + LANES), BF16),
        ],
        swapped, part, near_tok,
        scratch=[pltpu.VMEM((experts, per_expert, count), F32)],
        flops=4 * slots * count * half,
    )
    came = lax.ppermute(send, "core", SWAP)
    keep, mix, w_other_second = call(
        functools.partial(keep_sums_kernel, other_rows),
        [((slots, half), F32), ((slots, count), BF16), ((half - other_rows, units), BF16)],
        logits, weights, near_tok, w_in,
        copies=1, in_hbm=(3,), stay=(2,), flops=2 * slots * count * half,
    )
    (packed,) = call(
        chip_sum_kernel,
        [((experts, chips, per_expert, half + LANES), BF16)],
        keep, stats, came,
        limit=16 << 20,
    )
    both = ("expert", "chip")
    flat = packed.reshape((experts * chips,) + packed.shape[2:])
    mine = lax.all_to_all(flat, both, split_axis=0, concat_axis=0, tiled=True)
    swapped = lax.ppermute(mine, "core", SWAP)
    acc, w_near = call(
        own_hidden_kernel,
        [((slots, units), F32), ((near_units, width), BF16)],
        mine.reshape(packed.shape), w_own, w_out,
        copies=1, in_hbm=(2,), stay=(1,), flops=2 * slots * half * units, limit=16 << 20,
    )
    w_other = (w_other_first, w_other_second)
    pieces = math.gcd((units - near_units) // LANES, 4)
    send, hidden, w_rest = call(
        send_terms_kernel,
        [((slots, half), BF16), ((slots, units), BF16), ((units - near_units, width), BF16)],
        acc, swapped.reshape(packed.shape), *w_other, w_near, w_out,
        copies=pieces, in_hbm=(5,), stay=(2,), flops=4 * slots * half * units, limit=16 << 20,
    )
    came = lax.ppermute(send, "core", SWAP)
    (keep,) = call(
        keep_terms_kernel,
        [((slots, half), F32)],
        hidden, w_near, w_rest,
        flops=2 * slots * half * units,
    )
    (packed,) = call(
        pair_sum_kernel, [((experts, chips, per_expert, half), BF16)], keep, came, limit=16 << 20
    )
    flat = packed.reshape((experts * chips,) + packed.shape[2:])
    mine = lax.all_to_all(flat, both, split_axis=0, concat_axis=0, tiled=True)
    swapped = lax.ppermute(mine, "core", SWAP)
    (own_half,) = call(
        own_mix_kernel,
        [((count, half), BF16)],
        mix, mine.reshape(packed.shape),
        stay=(0,), flops=2 * slots * count * half, limit=16 << 20,
    )
    mixed = pl.pallas_call(
        mix_kernel,
        out_shape=jax.ShapeDtypeStruct((count, width), BF16),
        in_specs=[pl.BlockSpec(memory_space=pltpu.VMEM)] * 3,
        out_specs=pl.BlockSpec(memory_space=pltpu.HBM),
        scratch_shapes=[pltpu.VMEM((count, half), BF16), pltpu.SemaphoreType.DMA((2,))],
        compiler_params=pltpu.CompilerParams(vmem_limit_bytes=16 << 20),
        cost_estimate=pl.CostEstimate(
            flops=2 * slots * count * half, bytes_accessed=2 * count * width, transcendentals=0
        ),
    )(mix, swapped.reshape(packed.shape), own_half)
    return mixed[None]


def solution(mesh):
    sizes, names = [], []
    for name in mesh.axis_names:
        if name == "seq":
            sizes += [mesh.shape[name] // 2, 2]
            names += ["chip", "core"]
        else:
            sizes.append(mesh.shape[name])
            names.append(name)
    split = Mesh(mesh.devices.reshape(sizes), tuple(names))
    seq = ("chip", "core")
    placed = (
        P("expert", seq, None),
        P(None, "expert"),
        P("expert", None, seq),
        P("expert", seq, None),
    )
    return jax.shard_map(
        on_device, mesh=split, in_specs=placed, out_specs=P("expert", seq, None), check_vma=False
    )
```

```python
import functools
import math

import jax
import jax.numpy as jnp
from jax import lax
from jax.experimental import pallas as pl
from jax.experimental.pallas import tpu as pltpu
from jax.sharding import Mesh, PartitionSpec as P

F32 = jnp.float32
BF16 = jnp.bfloat16
LANES = 128
SWAP = ((0, 1), (1, 0))
ROWS_BY_ROWS = (((1,), (1,)), ((), ()))


def column_halves(half):
    core = lax.axis_index("core")
    own = pl.ds(pl.multiple_of(core * half, LANES), half)
    other = pl.ds(pl.multiple_of((1 - core) * half, LANES), half)
    return own, other


def three_terms(value):
    first = value.astype(BF16).astype(F32)
    rest = value - first
    second = rest.astype(BF16).astype(F32)
    return first, second, rest - second


def stats_tile(top, total):
    shape = top.shape[:-1] + (LANES,)
    lane = lax.broadcasted_iota(jnp.int32, shape, len(shape) - 1)
    tile = jnp.zeros(shape, F32)
    for place, term in enumerate(three_terms(top) + three_terms(total)):
        tile = jnp.where(lane == place, term, tile)
    return tile


def read_stats(tile):
    top = tile[..., 0:1] + tile[..., 1:2] + tile[..., 2:3]
    total = tile[..., 3:4] + tile[..., 4:5] + tile[..., 5:6]
    return top, total


def copy_parts(sem, pairs):
    copies = [pltpu.make_async_copy(src, dst, sem.at[i]) for i, (src, dst) in enumerate(pairs)]
    for copy in copies:
        copy.start()
    return copies


def block_rows(start, count):
    return pl.ds(pl.multiple_of(start, LANES), count)


def held_masks(experts):
    return [((experts - 2 * k) % experts, 2 * k + 1) for k in range(experts // 2)]


def gather_keys(keys, experts, chips):
    axes = ("chip", "core", "expert")
    blocks = []
    for masks in held_masks(experts):
        pairs = [
            (((chip * 2 + core) * experts + e), ((chip * 2 + core) * experts + (e ^ mask)))
            for chip in range(chips)
            for core, mask in enumerate(masks)
            if mask
            for e in range(experts)
        ]
        blocks.append(lax.ppermute(keys, axes, pairs))
    return blocks


def stack_kernel(*refs):
    keys_ref, *blocks, out_ref = refs
    out_ref[0] = jnp.where(lax.axis_index("core") == 0, keys_ref[...], blocks[0][...])
    for k, block in enumerate(blocks[1:]):
        out_ref[k + 1] = block[...]


def first_fetch_kernel(tok_ref, w_in_ref, near_tok, near_w, sem):
    rows = near_w.shape[0]
    start = lax.axis_index("core") * rows
    pairs = [(tok_ref, near_tok), (w_in_ref.at[block_rows(start, rows)], near_w)]
    for copy in copy_parts(sem, pairs):
        copy.wait()


def held_logits(stack_ref, tok_ref):
    blocks, rows, width = stack_ref.shape
    return lax.dot_general(
        stack_ref[...].reshape(blocks * rows, width), tok_ref[...], ROWS_BY_ROWS,
        preferred_element_type=F32,
    )


def held_logits_kernel(stack_ref, tok_ref, w_in_ref, part_ref, near_w, sem):
    start = (1 - lax.axis_index("core")) * (w_in_ref.shape[0] // 2)
    copies = copy_parts(sem, [(w_in_ref.at[block_rows(start, near_w.shape[0])], near_w)])
    part_ref[...] = held_logits(stack_ref, tok_ref)
    for copy in copies:
        copy.wait()


def send_sums_kernel(
    swapped_ref, part_ref, tok_ref, logits_ref, weights_ref, stats_ref, send_ref, sorted_ref
):
    half = tok_ref.shape[1] // 2
    _, other = column_halves(half)
    experts, rows, count = sorted_ref.shape
    expert, core = lax.axis_index("expert"), lax.axis_index("core")
    theirs = held_logits(swapped_ref, tok_ref)
    for k, (even, odd) in enumerate(held_masks(experts)):
        held = slice(k * rows, (k + 1) * rows)
        sorted_ref[expert ^ jnp.where(core == 0, even, odd)] = part_ref[held, :]
        sorted_ref[expert ^ jnp.where(core == 0, odd, even)] = theirs[held, :]
    logits = sorted_ref[...].reshape(experts * rows, count)
    logits_ref[...] = logits
    top = jnp.max(logits, axis=1, keepdims=True)
    weights = jnp.exp(logits - top).astype(BF16)
    weights_ref[...] = weights
    total = jnp.sum(weights.astype(F32), axis=1, keepdims=True)
    send_ref[:, :half] = jnp.dot(weights, tok_ref[:, other], preferred_element_type=F32).astype(BF16)
    send_ref[:, half:] = stats_tile(top, total).astype(BF16)
    lane = lax.broadcasted_iota(jnp.int32, stats_ref.shape, 1)
    stats_ref[...] = jnp.where(lane == 0, top, total)


def keep_sums_kernel(
    skip, logits_ref, weights_ref, tok_ref, w_in_ref, keep_ref, mix_ref, near_w, sem
):
    half = keep_ref.shape[1]
    start = (1 - lax.axis_index("core")) * half + skip
    copies = copy_parts(sem, [(w_in_ref.at[block_rows(start, near_w.shape[0])], near_w)])
    own, _ = column_halves(half)
    keep_ref[...] = jnp.dot(weights_ref[...], tok_ref[:, own], preferred_element_type=F32)
    logits = logits_ref[...]
    raised = jnp.exp(logits - jnp.max(logits, axis=0, keepdims=True))
    mix_ref[...] = (raised / jnp.sum(raised, axis=0, keepdims=True)).astype(BF16)
    for copy in copies:
        copy.wait()


def chip_sum_kernel(keep_ref, stats_ref, came_ref, out_ref):
    half = keep_ref.shape[1]
    experts, chips, rows, _ = out_ref.shape
    top, total = stats_ref[:, 0:1], stats_ref[:, 1:2]
    came_top, came_total = read_stats(came_ref[:, half:].astype(F32))
    new_top = jnp.maximum(top, came_top)
    scale, came_scale = jnp.exp(top - new_top), jnp.exp(came_top - new_top)
    sums = (keep_ref[...] * scale + came_ref[:, :half].astype(F32) * came_scale).astype(BF16)
    tile = stats_tile(new_top, total * scale + came_total * came_scale).astype(BF16)
    sums = sums.reshape(experts, rows, half)
    tile = tile.reshape(experts, rows, LANES)
    for chip in range(chips):
        out_ref[:, chip, :, :half] = sums
        out_ref[:, chip, :, half:] = tile


def slot_inputs_of(ref):
    seqs, chips, rows, width = ref.shape
    half = width - LANES
    stats = [read_stats(ref[:, chip, :, half:].astype(F32)) for chip in range(chips)]
    top = functools.reduce(jnp.maximum, [s[0] for s in stats])
    scales = [jnp.exp(s[0] - top) for s in stats]
    total = sum(scale * s[1] for scale, s in zip(scales, stats))
    summed = sum(ref[:, chip, :, :half].astype(F32) * scales[chip] for chip in range(chips))
    return (summed / total).reshape(seqs * rows, half).astype(BF16)


def row_blocks_dot(left, blocks):
    start, total = 0, 0
    for block in blocks:
        rows = block.shape[0]
        total += jnp.dot(left[:, start : start + rows], block[...], preferred_element_type=F32)
        start += rows
    return total


def own_hidden_kernel(
    mine_ref, w_own_ref, w_out_ref, acc_ref, near_out, sem
):
    copies = copy_parts(sem, [(w_out_ref.at[pl.ds(0, near_out.shape[0])], near_out)])
    acc_ref[...] = row_blocks_dot(slot_inputs_of(mine_ref), (w_own_ref,))
    for copy in copies:
        copy.wait()


def send_terms_kernel(
    acc_ref, swapped_ref, w_first_ref, w_second_ref, w_near_ref, w_out_ref,
    send_ref, hidden_ref, rest, sem,
):
    _, other = column_halves(w_out_ref.shape[1] // 2)
    near, pieces = w_near_ref.shape[0], sem.shape[0]
    step = rest.shape[0] // pieces
    copies = copy_parts(sem, [
        (w_out_ref.at[pl.ds(near + i * step, step)], rest.at[pl.ds(i * step, step)])
        for i in range(pieces)
    ])
    summed = acc_ref[...] + row_blocks_dot(slot_inputs_of(swapped_ref), (w_first_ref, w_second_ref))
    hidden = jax.nn.gelu(summed, approximate=True).astype(BF16)
    hidden_ref[...] = hidden
    sent = jnp.dot(hidden[:, :near], w_near_ref[:, other], preferred_element_type=F32)
    for i, copy in enumerate(copies):
        copy.wait()
        rows = pl.ds(near + i * step, step)
        sent += jnp.dot(
            hidden_ref[:, rows], rest[pl.ds(i * step, step), other], preferred_element_type=F32
        )
    send_ref[...] = sent.astype(BF16)


def keep_terms_kernel(hidden_ref, w_near_ref, w_rest_ref, keep_ref):
    own, _ = column_halves(keep_ref.shape[1])
    near = w_near_ref.shape[0]
    keep_ref[...] = jnp.dot(
        hidden_ref[:, :near], w_near_ref[:, own], preferred_element_type=F32
    ) + jnp.dot(hidden_ref[:, near:], w_rest_ref[:, own], preferred_element_type=F32)


def pair_sum_kernel(keep_ref, came_ref, out_ref):
    seqs, chips, rows, half = out_ref.shape
    sums = (keep_ref[...] + came_ref[...].astype(F32)).astype(BF16).reshape(seqs, rows, half)
    for chip in range(chips):
        out_ref[:, chip] = sums


def mixed_half(mix_ref, ref):
    experts, chips, rows, half = ref.shape
    summed = sum(ref[:, chip].astype(F32) for chip in range(chips))
    slot_outputs = summed.reshape(experts * rows, half).astype(BF16)
    return lax.dot_general(
        mix_ref[...], slot_outputs, (((0,), (0,)), ((), ())), preferred_element_type=F32
    ).astype(BF16)


def own_mix_kernel(mix_ref, mine_ref, half_ref):
    half_ref[...] = mixed_half(mix_ref, mine_ref)


def mix_kernel(mix_ref, swapped_ref, half_ref, out_ref, rest, sem):
    own, other = column_halves(half_ref.shape[1])
    copies = copy_parts(sem, [(half_ref, out_ref.at[:, own])])
    rest[...] = mixed_half(mix_ref, swapped_ref)
    last = pltpu.make_async_copy(rest, out_ref.at[:, other], sem.at[1])
    last.start()
    copies[0].wait()
    last.wait()


def call(kernel, outs, *args, scratch=(), copies=0, in_hbm=(), stay=(), flops=0, limit=8 << 20):
    if copies:
        scratch = tuple(scratch) + (pltpu.SemaphoreType.DMA((copies,)),)
    shapes, out_specs = [], []
    for i, (shape, dtype) in enumerate(outs):
        shapes.append((pltpu.VMEM if i in stay else jax.ShapeDtypeStruct)(shape, dtype))
        out_specs.append(pl.BlockSpec(memory_space=pltpu.VMEM))
    return pl.pallas_call(
        kernel,
        out_shape=shapes,
        in_specs=[
            pl.BlockSpec(memory_space=pltpu.HBM if i in in_hbm else pltpu.VMEM)
            for i in range(len(args))
        ],
        out_specs=out_specs,
        scratch_shapes=list(scratch),
        compiler_params=pltpu.CompilerParams(vmem_limit_bytes=limit),
        cost_estimate=pl.CostEstimate(
            flops=flops,
            bytes_accessed=sum(math.prod(shape) * jnp.dtype(dtype).itemsize for shape, dtype in outs),
            transcendentals=0,
        ),
    )(*[
        pltpu.with_memory_space_constraint(a, pltpu.HBM) if i in in_hbm else a
        for i, a in enumerate(args)
    ])


def share(count, numerator, denominator):
    return max(LANES, count * numerator // denominator // LANES * LANES)


def on_device(tokens, slot_keys, w_in, w_out):
    token_rows, w_in, w_out = tokens[0], w_in[0], w_out[0]
    count, width = token_rows.shape
    half = width // 2
    per_expert = slot_keys.shape[1]
    experts, chips = lax.axis_size("expert"), lax.axis_size("chip")
    slots = experts * per_expert
    units = w_in.shape[1]
    other_rows = share(half, 1, 2)
    near_units = share(units, 1, 3)

    keys = slot_keys.T
    blocks = gather_keys(keys, experts, chips)
    near_tok, w_own = call(
        first_fetch_kernel,
        [(token_rows.shape, BF16), ((half, units), BF16)],
        token_rows, w_in,
        copies=2, in_hbm=(0, 1), stay=(0, 1),
    )
    *blocks, near_tok, w_own = lax.optimization_barrier((*blocks, near_tok, w_own))
    (stack,) = call(
        stack_kernel, [((experts // 2, per_expert, width), BF16)], keys, *blocks
    )
    swapped = lax.ppermute(stack, "core", SWAP)
    part, w_other_first = call(
        held_logits_kernel,
        [((slots // 2, count), F32), ((other_rows, units), BF16)],
        stack, near_tok, w_in,
        copies=1, in_hbm=(2,), stay=(1,), flops=2 * slots * count * half,
    )
    logits, weights, stats, send = call(
        send_sums_kernel,
        [
            ((slots, count), F32),
            ((slots, count), BF16),
            ((slots, LANES), F32),
            ((slots, half + LANES), BF16),
        ],
        swapped, part, near_tok,
        scratch=[pltpu.VMEM((experts, per_expert, count), F32)],
        flops=4 * slots * count * half,
    )
    came = lax.ppermute(send, "core", SWAP)
    keep, mix, w_other_second = call(
        functools.partial(keep_sums_kernel, other_rows),
        [((slots, half), F32), ((slots, count), BF16), ((half - other_rows, units), BF16)],
        logits, weights, near_tok, w_in,
        copies=1, in_hbm=(3,), stay=(2,), flops=2 * slots * count * half,
    )
    (packed,) = call(
        chip_sum_kernel,
        [((experts, chips, per_expert, half + LANES), BF16)],
        keep, stats, came,
        limit=16 << 20,
    )
    both = ("expert", "chip")
    flat = packed.reshape((experts * chips,) + packed.shape[2:])
    mine = lax.all_to_all(flat, both, split_axis=0, concat_axis=0, tiled=True)
    swapped = lax.ppermute(mine, "core", SWAP)
    acc, w_near = call(
        own_hidden_kernel,
        [((slots, units), F32), ((near_units, width), BF16)],
        mine.reshape(packed.shape), w_own, w_out,
        copies=1, in_hbm=(2,), stay=(1,), flops=2 * slots * half * units, limit=16 << 20,
    )
    w_other = (w_other_first, w_other_second)
    pieces = math.gcd((units - near_units) // LANES, 4)
    send, hidden, w_rest = call(
        send_terms_kernel,
        [((slots, half), BF16), ((slots, units), BF16), ((units - near_units, width), BF16)],
        acc, swapped.reshape(packed.shape), *w_other, w_near, w_out,
        copies=pieces, in_hbm=(5,), stay=(2,), flops=4 * slots * half * units, limit=16 << 20,
    )
    came = lax.ppermute(send, "core", SWAP)
    (keep,) = call(
        keep_terms_kernel,
        [((slots, half), F32)],
        hidden, w_near, w_rest,
        flops=2 * slots * half * units,
    )
    (packed,) = call(
        pair_sum_kernel, [((experts, chips, per_expert, half), BF16)], keep, came, limit=16 << 20
    )
    flat = packed.reshape((experts * chips,) + packed.shape[2:])
    mine = lax.all_to_all(flat, both, split_axis=0, concat_axis=0, tiled=True)
    swapped = lax.ppermute(mine, "core", SWAP)
    (own_half,) = call(
        own_mix_kernel,
        [((count, half), BF16)],
        mix, mine.reshape(packed.shape),
        stay=(0,), flops=2 * slots * count * half, limit=16 << 20,
    )
    mixed = pl.pallas_call(
        mix_kernel,
        out_shape=jax.ShapeDtypeStruct((count, width), BF16),
        in_specs=[pl.BlockSpec(memory_space=pltpu.VMEM)] * 3,
        out_specs=pl.BlockSpec(memory_space=pltpu.HBM),
        scratch_shapes=[pltpu.VMEM((count, half), BF16), pltpu.SemaphoreType.DMA((2,))],
        compiler_params=pltpu.CompilerParams(vmem_limit_bytes=16 << 20),
        cost_estimate=pl.CostEstimate(
            flops=2 * slots * count * half, bytes_accessed=2 * count * width, transcendentals=0
        ),
    )(mix, swapped.reshape(packed.shape), own_half)
    return mixed[None]


def solution(mesh):
    sizes, names = [], []
    for name in mesh.axis_names:
        if name == "seq":
            sizes += [mesh.shape[name] // 2, 2]
            names += ["chip", "core"]
        else:
            sizes.append(mesh.shape[name])
            names.append(name)
    split = Mesh(mesh.devices.reshape(sizes), tuple(names))
    seq = ("chip", "core")
    placed = (
        P("expert", seq, None),
        P(None, "expert"),
        P("expert", None, seq),
        P("expert", seq, None),
    )
    return jax.shard_map(
        on_device, mesh=split, in_specs=placed, out_specs=P("expert", seq, None), check_vma=False
    )
```

```python
import functools
import math

import jax
import jax.numpy as jnp
from jax import lax
from jax.experimental import pallas as pl
from jax.experimental.pallas import tpu as pltpu
from jax.sharding import Mesh, PartitionSpec as P

F32 = jnp.float32
BF16 = jnp.bfloat16
LANES = 128
COVER_FLOPS = 10**9
SWAP = ((0, 1), (1, 0))
ROWS_BY_ROWS = (((1,), (1,)), ((), ()))


def column_halves(half):
    core = lax.axis_index("core")
    own = pl.ds(pl.multiple_of(core * half, LANES), half)
    other = pl.ds(pl.multiple_of((1 - core) * half, LANES), half)
    return own, other


def row_halves(ref):
    return column_halves(ref.shape[0] // 2)


def three_terms(value):
    first = value.astype(BF16).astype(F32)
    rest = value - first
    second = rest.astype(BF16).astype(F32)
    return first, second, rest - second


def stats_tile(top, total):
    shape = top.shape[:-1] + (LANES,)
    lane = lax.broadcasted_iota(jnp.int32, shape, len(shape) - 1)
    tile = jnp.zeros(shape, F32)
    for place, term in enumerate(three_terms(top) + three_terms(total)):
        tile = jnp.where(lane == place, term, tile)
    return tile


def read_stats(tile):
    top = tile[..., 0:1] + tile[..., 1:2] + tile[..., 2:3]
    total = tile[..., 3:4] + tile[..., 4:5] + tile[..., 5:6]
    return top, total


def copy_parts(sem, pairs):
    copies = [pltpu.make_async_copy(src, dst, sem.at[i]) for i, (src, dst) in enumerate(pairs)]
    for copy in copies:
        copy.start()
    return copies


def block_rows(start, count):
    return pl.ds(pl.multiple_of(start, LANES), count)


def held_masks(experts):
    return [((experts - 2 * k) % experts, 2 * k + 1) for k in range(experts // 2)]


def gather_keys(keys, experts, chips):
    axes = ("chip", "core", "expert")
    blocks = []
    for masks in held_masks(experts):
        pairs = [
            (((chip * 2 + core) * experts + e), ((chip * 2 + core) * experts + (e ^ mask)))
            for chip in range(chips)
            for core, mask in enumerate(masks)
            for e in range(experts)
        ]
        blocks.append(lax.ppermute(keys, axes, pairs))
    return blocks


def stack_kernel(*refs):
    for k, block in enumerate(refs[:-1]):
        refs[-1][k] = block[...]


def fetch_kernel(far_ref, near_ref, sem):
    copy = pltpu.make_async_copy(far_ref, near_ref, sem.at[0])
    copy.start()
    copy.wait()


def held_logits(stack_ref, tok_ref):
    blocks, rows, width = stack_ref.shape
    return lax.dot_general(
        stack_ref[...].reshape(blocks * rows, width), tok_ref[...], ROWS_BY_ROWS,
        preferred_element_type=F32,
    )


def held_logits_kernel(stack_ref, tok_ref, part_ref):
    part_ref[...] = held_logits(stack_ref, tok_ref)


def send_sums_kernel(
    swapped_ref, part_ref, tok_ref, logits_ref, weights_ref, stats_ref, send_ref, sorted_ref
):
    half = tok_ref.shape[1] // 2
    _, other = column_halves(half)
    experts, rows, count = sorted_ref.shape
    expert, core = lax.axis_index("expert"), lax.axis_index("core")
    theirs = held_logits(swapped_ref, tok_ref)
    for k, (even, odd) in enumerate(held_masks(experts)):
        held = slice(k * rows, (k + 1) * rows)
        sorted_ref[expert ^ jnp.where(core == 0, even, odd)] = part_ref[held, :]
        sorted_ref[expert ^ jnp.where(core == 0, odd, even)] = theirs[held, :]
    logits = sorted_ref[...].reshape(experts * rows, count)
    logits_ref[...] = logits
    top = jnp.max(logits, axis=1, keepdims=True)
    weights = jnp.exp(logits - top).astype(BF16)
    weights_ref[...] = weights
    total = jnp.sum(weights.astype(F32), axis=1, keepdims=True)
    send_ref[:, :half] = jnp.dot(weights, tok_ref[:, other], preferred_element_type=F32).astype(BF16)
    send_ref[:, half:] = stats_tile(top, total).astype(BF16)
    lane = lax.broadcasted_iota(jnp.int32, stats_ref.shape, 1)
    stats_ref[...] = jnp.where(lane == 0, top, total)


def keep_sums_kernel(logits_ref, weights_ref, tok_ref, keep_ref, mix_ref):
    own, _ = column_halves(keep_ref.shape[1])
    keep_ref[...] = jnp.dot(weights_ref[...], tok_ref[:, own], preferred_element_type=F32)
    logits = logits_ref[...]
    raised = jnp.exp(logits - jnp.max(logits, axis=0, keepdims=True))
    mix_ref[...] = (raised / jnp.sum(raised, axis=0, keepdims=True)).astype(BF16)


def chip_sum_kernel(keep_ref, stats_ref, came_ref, out_ref):
    half = keep_ref.shape[1]
    experts, chips, rows, _ = out_ref.shape
    top, total = stats_ref[:, 0:1], stats_ref[:, 1:2]
    came_top, came_total = read_stats(came_ref[:, half:].astype(F32))
    new_top = jnp.maximum(top, came_top)
    scale, came_scale = jnp.exp(top - new_top), jnp.exp(came_top - new_top)
    sums = (keep_ref[...] * scale + came_ref[:, :half].astype(F32) * came_scale).astype(BF16)
    tile = stats_tile(new_top, total * scale + came_total * came_scale).astype(BF16)
    sums = sums.reshape(experts, rows, half)
    tile = tile.reshape(experts, rows, LANES)
    for chip in range(chips):
        out_ref[:, chip, :, :half] = sums
        out_ref[:, chip, :, half:] = tile


def slot_inputs_of(ref):
    seqs, chips, rows, width = ref.shape
    half = width - LANES
    stats = [read_stats(ref[:, chip, :, half:].astype(F32)) for chip in range(chips)]
    top = functools.reduce(jnp.maximum, [s[0] for s in stats])
    scales = [jnp.exp(s[0] - top) for s in stats]
    total = sum(scale * s[1] for scale, s in zip(scales, stats))
    summed = sum(ref[:, chip, :, :half].astype(F32) * scales[chip] for chip in range(chips))
    return (summed / total).reshape(seqs * rows, half).astype(BF16)


def own_hidden_kernel(mine_ref, w_in_ref, acc_ref):
    own, _ = row_halves(w_in_ref)
    acc_ref[...] = jnp.dot(slot_inputs_of(mine_ref), w_in_ref[own, :], preferred_element_type=F32)


def send_terms_kernel(acc_ref, swapped_ref, w_in_ref, w_out_ref, send_ref, hidden_ref):
    _, other = row_halves(w_in_ref)
    summed = acc_ref[...] + jnp.dot(
        slot_inputs_of(swapped_ref), w_in_ref[other, :], preferred_element_type=F32
    )
    hidden = jax.nn.gelu(summed, approximate=True).astype(BF16)
    hidden_ref[...] = hidden
    _, other = column_halves(send_ref.shape[1])
    send_ref[...] = jnp.dot(hidden, w_out_ref[:, other], preferred_element_type=F32).astype(BF16)


def keep_terms_kernel(hidden_ref, w_out_ref, keep_ref):
    own, _ = column_halves(keep_ref.shape[1])
    keep_ref[...] = jnp.dot(hidden_ref[...], w_out_ref[:, own], preferred_element_type=F32)


def pair_sum_kernel(keep_ref, came_ref, out_ref):
    seqs, chips, rows, half = out_ref.shape
    sums = (keep_ref[...] + came_ref[...].astype(F32)).astype(BF16).reshape(seqs, rows, half)
    for chip in range(chips):
        out_ref[:, chip] = sums


def mixed_half(mix_ref, ref):
    experts, chips, rows, half = ref.shape
    summed = sum(ref[:, chip].astype(F32) for chip in range(chips))
    slot_outputs = summed.reshape(experts * rows, half).astype(BF16)
    return lax.dot_general(
        mix_ref[...], slot_outputs, (((0,), (0,)), ((), ())), preferred_element_type=F32
    ).astype(BF16)


def own_mix_kernel(mix_ref, mine_ref, half_ref):
    half_ref[...] = mixed_half(mix_ref, mine_ref)


def mix_kernel(mix_ref, swapped_ref, half_ref, out_ref, rest, sem):
    own, other = column_halves(half_ref.shape[1])
    copies = copy_parts(sem, [(half_ref, out_ref.at[:, own])])
    rest[...] = mixed_half(mix_ref, swapped_ref)
    last = pltpu.make_async_copy(rest, out_ref.at[:, other], sem.at[1])
    last.start()
    copies[0].wait()
    last.wait()


def call(kernel, outs, *args, scratch=(), copies=0, in_hbm=(), stay=(), flops=0, limit=8 << 20):
    if copies:
        scratch = tuple(scratch) + (pltpu.SemaphoreType.DMA((copies,)),)
    shapes, out_specs = [], []
    for i, (shape, dtype) in enumerate(outs):
        shapes.append((pltpu.VMEM if i in stay else jax.ShapeDtypeStruct)(shape, dtype))
        out_specs.append(pl.BlockSpec(memory_space=pltpu.VMEM))
    return pl.pallas_call(
        kernel,
        out_shape=shapes,
        in_specs=[
            pl.BlockSpec(memory_space=pltpu.HBM if i in in_hbm else pltpu.VMEM)
            for i in range(len(args))
        ],
        out_specs=out_specs,
        scratch_shapes=list(scratch),
        compiler_params=pltpu.CompilerParams(vmem_limit_bytes=limit),
        cost_estimate=pl.CostEstimate(
            flops=flops,
            bytes_accessed=sum(math.prod(shape) * jnp.dtype(dtype).itemsize for shape, dtype in outs),
            transcendentals=0,
        ),
    )(*[
        pltpu.with_memory_space_constraint(a, pltpu.HBM) if i in in_hbm else a
        for i, a in enumerate(args)
    ])


def on_device(tokens, slot_keys, w_in, w_out):
    token_rows, w_in, w_out = tokens[0], w_in[0], w_out[0]
    count, width = token_rows.shape
    half = width // 2
    per_expert = slot_keys.shape[1]
    experts, chips = lax.axis_size("expert"), lax.axis_size("chip")
    slots = experts * per_expert
    units = w_in.shape[1]

    keys = slot_keys.T
    blocks = gather_keys(keys, experts, chips)
    (token_rows,) = call(
        fetch_kernel, [(token_rows.shape, BF16)], token_rows, copies=1, in_hbm=(0,), stay=(0,)
    )
    *blocks, token_rows = lax.optimization_barrier((*blocks, token_rows))
    (stack,) = call(
        stack_kernel, [((experts // 2, per_expert, width), BF16)], *blocks
    )
    swapped = lax.ppermute(stack, "core", SWAP)
    (part,) = call(
        held_logits_kernel, [((slots // 2, count), F32)], stack, token_rows,
        flops=2 * slots * count * half,
    )
    logits, weights, stats, send = call(
        send_sums_kernel,
        [
            ((slots, count), F32),
            ((slots, count), BF16),
            ((slots, LANES), F32),
            ((slots, half + LANES), BF16),
        ],
        swapped, part, token_rows,
        scratch=[pltpu.VMEM((experts, per_expert, count), F32)],
        flops=4 * slots * count * half,
    )
    came = lax.ppermute(send, "core", SWAP)
    keep, mix = call(
        keep_sums_kernel,
        [((slots, half), F32), ((slots, count), BF16)],
        logits, weights, token_rows,
        flops=2 * slots * count * half,
    )
    (packed,) = call(
        chip_sum_kernel,
        [((experts, chips, per_expert, half + LANES), BF16)],
        keep, stats, came,
        flops=COVER_FLOPS, limit=16 << 20,
    )
    both = ("expert", "chip")
    flat = packed.reshape((experts * chips,) + packed.shape[2:])
    mine = lax.all_to_all(flat, both, split_axis=0, concat_axis=0, tiled=True)
    swapped = lax.ppermute(mine, "core", SWAP)
    (acc,) = call(
        own_hidden_kernel,
        [((slots, units), F32)],
        mine.reshape(packed.shape), w_in,
        flops=2 * slots * half * units, limit=16 << 20,
    )
    send, hidden = call(
        send_terms_kernel,
        [((slots, half), BF16), ((slots, units), BF16)],
        acc, swapped.reshape(packed.shape), w_in, w_out,
        flops=4 * slots * half * units, limit=16 << 20,
    )
    came = lax.ppermute(send, "core", SWAP)
    (keep,) = call(
        keep_terms_kernel, [((slots, half), F32)], hidden, w_out, flops=2 * slots * half * units
    )
    (packed,) = call(
        pair_sum_kernel, [((experts, chips, per_expert, half), BF16)], keep, came, limit=16 << 20
    )
    flat = packed.reshape((experts * chips,) + packed.shape[2:])
    mine = lax.all_to_all(flat, both, split_axis=0, concat_axis=0, tiled=True)
    swapped = lax.ppermute(mine, "core", SWAP)
    (own_half,) = call(
        own_mix_kernel,
        [((count, half), BF16)],
        mix, mine.reshape(packed.shape),
        stay=(0,), flops=2 * slots * count * half, limit=16 << 20,
    )
    mixed = pl.pallas_call(
        mix_kernel,
        out_shape=jax.ShapeDtypeStruct((count, width), BF16),
        in_specs=[pl.BlockSpec(memory_space=pltpu.VMEM)] * 3,
        out_specs=pl.BlockSpec(memory_space=pltpu.HBM),
        scratch_shapes=[pltpu.VMEM((count, half), BF16), pltpu.SemaphoreType.DMA((2,))],
        compiler_params=pltpu.CompilerParams(vmem_limit_bytes=16 << 20),
        cost_estimate=pl.CostEstimate(
            flops=2 * slots * count * half, bytes_accessed=2 * count * width, transcendentals=0
        ),
    )(mix, swapped.reshape(packed.shape), own_half)
    return mixed[None]


def solution(mesh):
    sizes, names = [], []
    for name in mesh.axis_names:
        if name == "seq":
            sizes += [mesh.shape[name] // 2, 2]
            names += ["chip", "core"]
        else:
            sizes.append(mesh.shape[name])
            names.append(name)
    split = Mesh(mesh.devices.reshape(sizes), tuple(names))
    seq = ("chip", "core")
    placed = (
        P("expert", seq, None),
        P(None, "expert"),
        P("expert", None, seq),
        P("expert", seq, None),
    )
    return jax.shard_map(
        on_device, mesh=split, in_specs=placed, out_specs=P("expert", seq, None), check_vma=False
    )
```

```python
import functools
import math

import jax
import jax.numpy as jnp
from jax import lax
from jax.experimental import pallas as pl
from jax.experimental.pallas import tpu as pltpu
from jax.sharding import Mesh, PartitionSpec as P

F32 = jnp.float32
BF16 = jnp.bfloat16
LANES = 128
COVER_FLOPS = 10**9
SWAP = ((0, 1), (1, 0))
ROWS_BY_ROWS = (((1,), (1,)), ((), ()))


def column_halves(half):
    high = lax.axis_index("expert") // (lax.axis_size("expert") // 2)
    side = (lax.axis_index("core") + high) % 2
    own = pl.ds(pl.multiple_of(side * half, LANES), half)
    other = pl.ds(pl.multiple_of((1 - side) * half, LANES), half)
    return own, other


def row_halves(ref):
    return column_halves(ref.shape[0] // 2)


def three_terms(value):
    first = value.astype(BF16).astype(F32)
    rest = value - first
    second = rest.astype(BF16).astype(F32)
    return first, second, rest - second


def stats_tile(top, total):
    shape = top.shape[:-1] + (LANES,)
    lane = lax.broadcasted_iota(jnp.int32, shape, len(shape) - 1)
    tile = jnp.zeros(shape, F32)
    for place, term in enumerate(three_terms(top) + three_terms(total)):
        tile = jnp.where(lane == place, term, tile)
    return tile


def read_stats(tile):
    top = tile[..., 0:1] + tile[..., 1:2] + tile[..., 2:3]
    total = tile[..., 3:4] + tile[..., 4:5] + tile[..., 5:6]
    return top, total


def copy_parts(sem, pairs):
    copies = [pltpu.make_async_copy(src, dst, sem.at[i]) for i, (src, dst) in enumerate(pairs)]
    for copy in copies:
        copy.start()
    return copies


def block_rows(start, count):
    return pl.ds(pl.multiple_of(start, LANES), count)


def held_masks(experts):
    odd = list(range(1, experts, 2))
    odd[-2:] = odd[:-3:-1]
    return [((experts - 2 * k) % experts, mask) for k, mask in enumerate(odd)]


def gather_keys(keys, experts, chips):
    axes = ("chip", "core", "expert")
    blocks = []
    for masks in held_masks(experts):
        pairs = [
            (((chip * 2 + core) * experts + e), ((chip * 2 + core) * experts + (e ^ mask)))
            for chip in range(chips)
            for core, mask in enumerate(masks)
            for e in range(experts)
        ]
        blocks.append(lax.ppermute(keys, axes, pairs))
    return blocks


def stack_kernel(*refs):
    for k, block in enumerate(refs[:-1]):
        refs[-1][k] = block[...]


def fetch_kernel(far_ref, near_ref, sem):
    copy = pltpu.make_async_copy(far_ref, near_ref, sem.at[0])
    copy.start()
    copy.wait()


def held_logits(stack_ref, tok_ref):
    blocks, rows, width = stack_ref.shape
    return lax.dot_general(
        stack_ref[...].reshape(blocks * rows, width), tok_ref[...], ROWS_BY_ROWS,
        preferred_element_type=F32,
    )


def held_logits_kernel(stack_ref, tok_ref, part_ref):
    part_ref[...] = held_logits(stack_ref, tok_ref)


def send_sums_kernel(
    swapped_ref, part_ref, tok_ref, logits_ref, weights_ref, stats_ref, send_ref, sorted_ref
):
    half = tok_ref.shape[1] // 2
    _, other = column_halves(half)
    experts, rows, count = sorted_ref.shape
    expert, core = lax.axis_index("expert"), lax.axis_index("core")
    theirs = held_logits(swapped_ref, tok_ref)
    for k, (even, odd) in enumerate(held_masks(experts)):
        held = slice(k * rows, (k + 1) * rows)
        sorted_ref[expert ^ jnp.where(core == 0, even, odd)] = part_ref[held, :]
        sorted_ref[expert ^ jnp.where(core == 0, odd, even)] = theirs[held, :]
    logits = sorted_ref[...].reshape(experts * rows, count)
    logits_ref[...] = logits
    top = jnp.max(logits, axis=1, keepdims=True)
    weights = jnp.exp(logits - top).astype(BF16)
    weights_ref[...] = weights
    total = jnp.sum(weights.astype(F32), axis=1, keepdims=True)
    send_ref[:, :half] = jnp.dot(weights, tok_ref[:, other], preferred_element_type=F32).astype(BF16)
    send_ref[:, half:] = stats_tile(top, total).astype(BF16)
    lane = lax.broadcasted_iota(jnp.int32, stats_ref.shape, 1)
    stats_ref[...] = jnp.where(lane == 0, top, total)


def keep_sums_kernel(logits_ref, weights_ref, tok_ref, keep_ref, mix_ref):
    own, _ = column_halves(keep_ref.shape[1])
    keep_ref[...] = jnp.dot(weights_ref[...], tok_ref[:, own], preferred_element_type=F32)
    logits = logits_ref[...]
    raised = jnp.exp(logits - jnp.max(logits, axis=0, keepdims=True))
    mix_ref[...] = (raised / jnp.sum(raised, axis=0, keepdims=True)).astype(BF16)


def chip_sum_kernel(keep_ref, stats_ref, came_ref, out_ref):
    half = keep_ref.shape[1]
    experts, chips, rows, _ = out_ref.shape
    top, total = stats_ref[:, 0:1], stats_ref[:, 1:2]
    came_top, came_total = read_stats(came_ref[:, half:].astype(F32))
    new_top = jnp.maximum(top, came_top)
    scale, came_scale = jnp.exp(top - new_top), jnp.exp(came_top - new_top)
    sums = (keep_ref[...] * scale + came_ref[:, :half].astype(F32) * came_scale).astype(BF16)
    tile = stats_tile(new_top, total * scale + came_total * came_scale).astype(BF16)
    sums = sums.reshape(experts, rows, half)
    tile = tile.reshape(experts, rows, LANES)
    for chip in range(chips):
        out_ref[:, chip, :, :half] = sums
        out_ref[:, chip, :, half:] = tile


def slot_inputs_of(ref):
    seqs, chips, rows, width = ref.shape
    half = width - LANES
    stats = [read_stats(ref[:, chip, :, half:].astype(F32)) for chip in range(chips)]
    top = functools.reduce(jnp.maximum, [s[0] for s in stats])
    scales = [jnp.exp(s[0] - top) for s in stats]
    total = sum(scale * s[1] for scale, s in zip(scales, stats))
    summed = sum(ref[:, chip, :, :half].astype(F32) * scales[chip] for chip in range(chips))
    return (summed / total).reshape(seqs * rows, half).astype(BF16)


def own_hidden_kernel(mine_ref, w_in_ref, acc_ref):
    own, _ = row_halves(w_in_ref)
    acc_ref[...] = jnp.dot(slot_inputs_of(mine_ref), w_in_ref[own, :], preferred_element_type=F32)


def send_terms_kernel(acc_ref, swapped_ref, w_in_ref, w_out_ref, send_ref, hidden_ref):
    _, other = row_halves(w_in_ref)
    summed = acc_ref[...] + jnp.dot(
        slot_inputs_of(swapped_ref), w_in_ref[other, :], preferred_element_type=F32
    )
    hidden = jax.nn.gelu(summed, approximate=True).astype(BF16)
    hidden_ref[...] = hidden
    _, other = column_halves(send_ref.shape[1])
    send_ref[...] = jnp.dot(hidden, w_out_ref[:, other], preferred_element_type=F32).astype(BF16)


def keep_terms_kernel(hidden_ref, w_out_ref, keep_ref):
    own, _ = column_halves(keep_ref.shape[1])
    keep_ref[...] = jnp.dot(hidden_ref[...], w_out_ref[:, own], preferred_element_type=F32)


def pair_sum_kernel(keep_ref, came_ref, out_ref):
    seqs, chips, rows, half = out_ref.shape
    sums = (keep_ref[...] + came_ref[...].astype(F32)).astype(BF16).reshape(seqs, rows, half)
    for chip in range(chips):
        out_ref[:, chip] = sums


def mixed_half(mix_ref, ref):
    experts, chips, rows, half = ref.shape
    summed = sum(ref[:, chip].astype(F32) for chip in range(chips))
    slot_outputs = summed.reshape(experts * rows, half).astype(BF16)
    return lax.dot_general(
        mix_ref[...], slot_outputs, (((0,), (0,)), ((), ())), preferred_element_type=F32
    ).astype(BF16)


def own_mix_kernel(mix_ref, mine_ref, half_ref):
    half_ref[...] = mixed_half(mix_ref, mine_ref)


def mix_kernel(mix_ref, swapped_ref, half_ref, out_ref, rest, sem):
    own, other = column_halves(half_ref.shape[1])
    copies = copy_parts(sem, [(half_ref, out_ref.at[:, own])])
    rest[...] = mixed_half(mix_ref, swapped_ref)
    last = pltpu.make_async_copy(rest, out_ref.at[:, other], sem.at[1])
    last.start()
    copies[0].wait()
    last.wait()


def call(kernel, outs, *args, scratch=(), copies=0, in_hbm=(), stay=(), flops=0, limit=8 << 20):
    if copies:
        scratch = tuple(scratch) + (pltpu.SemaphoreType.DMA((copies,)),)
    shapes, out_specs = [], []
    for i, (shape, dtype) in enumerate(outs):
        shapes.append((pltpu.VMEM if i in stay else jax.ShapeDtypeStruct)(shape, dtype))
        out_specs.append(pl.BlockSpec(memory_space=pltpu.VMEM))
    return pl.pallas_call(
        kernel,
        out_shape=shapes,
        in_specs=[
            pl.BlockSpec(memory_space=pltpu.HBM if i in in_hbm else pltpu.VMEM)
            for i in range(len(args))
        ],
        out_specs=out_specs,
        scratch_shapes=list(scratch),
        compiler_params=pltpu.CompilerParams(vmem_limit_bytes=limit),
        cost_estimate=pl.CostEstimate(
            flops=flops,
            bytes_accessed=sum(math.prod(shape) * jnp.dtype(dtype).itemsize for shape, dtype in outs),
            transcendentals=0,
        ),
    )(*[
        pltpu.with_memory_space_constraint(a, pltpu.HBM) if i in in_hbm else a
        for i, a in enumerate(args)
    ])


def on_device(tokens, slot_keys, w_in, w_out):
    token_rows, w_in, w_out = tokens[0], w_in[0], w_out[0]
    count, width = token_rows.shape
    half = width // 2
    per_expert = slot_keys.shape[1]
    experts, chips = lax.axis_size("expert"), lax.axis_size("chip")
    slots = experts * per_expert
    units = w_in.shape[1]

    keys = slot_keys.T
    blocks = gather_keys(keys, experts, chips)
    (token_rows,) = call(
        fetch_kernel, [(token_rows.shape, BF16)], token_rows, copies=1, in_hbm=(0,), stay=(0,)
    )
    *blocks, token_rows = lax.optimization_barrier((*blocks, token_rows))
    (stack,) = call(
        stack_kernel, [((experts // 2, per_expert, width), BF16)], *blocks
    )
    swapped = lax.ppermute(stack, "core", SWAP)
    (part,) = call(
        held_logits_kernel, [((slots // 2, count), F32)], stack, token_rows,
        flops=2 * slots * count * half,
    )
    logits, weights, stats, send = call(
        send_sums_kernel,
        [
            ((slots, count), F32),
            ((slots, count), BF16),
            ((slots, LANES), F32),
            ((slots, half + LANES), BF16),
        ],
        swapped, part, token_rows,
        scratch=[pltpu.VMEM((experts, per_expert, count), F32)],
        flops=4 * slots * count * half,
    )
    came = lax.ppermute(send, "core", SWAP)
    keep, mix = call(
        keep_sums_kernel,
        [((slots, half), F32), ((slots, count), BF16)],
        logits, weights, token_rows,
        flops=2 * slots * count * half,
    )
    (packed,) = call(
        chip_sum_kernel,
        [((experts, chips, per_expert, half + LANES), BF16)],
        keep, stats, came,
        flops=COVER_FLOPS, limit=16 << 20,
    )
    groups = [
        [
            (chip * 2 + (side + 2 * e // experts) % 2) * experts + e
            for e in range(experts)
            for chip in range(chips)
        ]
        for side in range(2)
    ]
    exchange = functools.partial(
        lax.all_to_all, axis_name=("chip", "core", "expert"), split_axis=0, concat_axis=0,
        axis_index_groups=groups, tiled=True,
    )
    flat = packed.reshape((experts * chips,) + packed.shape[2:])
    mine = exchange(flat)
    swapped = lax.ppermute(mine, "core", SWAP)
    (acc,) = call(
        own_hidden_kernel,
        [((slots, units), F32)],
        mine.reshape(packed.shape), w_in,
        flops=2 * slots * half * units, limit=16 << 20,
    )
    send, hidden = call(
        send_terms_kernel,
        [((slots, half), BF16), ((slots, units), BF16)],
        acc, swapped.reshape(packed.shape), w_in, w_out,
        flops=4 * slots * half * units, limit=16 << 20,
    )
    came = lax.ppermute(send, "core", SWAP)
    (keep,) = call(
        keep_terms_kernel, [((slots, half), F32)], hidden, w_out, flops=2 * slots * half * units
    )
    (packed,) = call(
        pair_sum_kernel, [((experts, chips, per_expert, half), BF16)], keep, came, limit=16 << 20
    )
    flat = packed.reshape((experts * chips,) + packed.shape[2:])
    mine = exchange(flat)
    swapped = lax.ppermute(mine, "core", SWAP)
    (own_half,) = call(
        own_mix_kernel,
        [((count, half), BF16)],
        mix, mine.reshape(packed.shape),
        stay=(0,), flops=2 * slots * count * half, limit=16 << 20,
    )
    mixed = pl.pallas_call(
        mix_kernel,
        out_shape=jax.ShapeDtypeStruct((count, width), BF16),
        in_specs=[pl.BlockSpec(memory_space=pltpu.VMEM)] * 3,
        out_specs=pl.BlockSpec(memory_space=pltpu.HBM),
        scratch_shapes=[pltpu.VMEM((count, half), BF16), pltpu.SemaphoreType.DMA((2,))],
        compiler_params=pltpu.CompilerParams(vmem_limit_bytes=16 << 20),
        cost_estimate=pl.CostEstimate(
            flops=2 * slots * count * half, bytes_accessed=2 * count * width, transcendentals=0
        ),
    )(mix, swapped.reshape(packed.shape), own_half)
    return mixed[None]


def solution(mesh):
    sizes, names = [], []
    for name in mesh.axis_names:
        if name == "seq":
            sizes += [mesh.shape[name] // 2, 2]
            names += ["chip", "core"]
        else:
            sizes.append(mesh.shape[name])
            names.append(name)
    split = Mesh(mesh.devices.reshape(sizes), tuple(names))
    seq = ("chip", "core")
    placed = (
        P("expert", seq, None),
        P(None, "expert"),
        P("expert", None, seq),
        P("expert", seq, None),
    )
    return jax.shard_map(
        on_device, mesh=split, in_specs=placed, out_specs=P("expert", seq, None), check_vma=False
    )
```

```python
import functools
import math
import random

import jax
import jax.numpy as jnp
from jax import lax
from jax.experimental import pallas as pl
from jax.experimental.pallas import tpu as pltpu
from jax.sharding import Mesh, PartitionSpec as P

F32 = jnp.float32
BF16 = jnp.bfloat16
LANES = 128
PEER_SEED = 19
COVER_FLOPS = 10**9
SWAP = ((0, 1), (1, 0))
ROWS_BY_ROWS = (((1,), (1,)), ((), ()))


def column_halves(half):
    high = lax.axis_index("expert") // (lax.axis_size("expert") // 2)
    side = (lax.axis_index("core") + high) % 2
    own = pl.ds(pl.multiple_of(side * half, LANES), half)
    other = pl.ds(pl.multiple_of((1 - side) * half, LANES), half)
    return own, other


def row_halves(ref):
    return column_halves(ref.shape[0] // 2)


def peer_order(experts, chips):
    order = [(e, chip) for e in range(experts) for chip in range(chips)]
    random.Random(PEER_SEED).shuffle(order)
    return order


def by_chip(experts, chips):
    places = {peer: place for place, peer in enumerate(peer_order(experts, chips))}
    return [[places[e, chip] for e in range(experts)] for chip in range(chips)]


def three_terms(value):
    first = value.astype(BF16).astype(F32)
    rest = value - first
    second = rest.astype(BF16).astype(F32)
    return first, second, rest - second


def stats_tile(top, total):
    shape = top.shape[:-1] + (LANES,)
    lane = lax.broadcasted_iota(jnp.int32, shape, len(shape) - 1)
    tile = jnp.zeros(shape, F32)
    for place, term in enumerate(three_terms(top) + three_terms(total)):
        tile = jnp.where(lane == place, term, tile)
    return tile


def read_stats(tile):
    top = tile[..., 0:1] + tile[..., 1:2] + tile[..., 2:3]
    total = tile[..., 3:4] + tile[..., 4:5] + tile[..., 5:6]
    return top, total


def copy_parts(sem, pairs):
    copies = [pltpu.make_async_copy(src, dst, sem.at[i]) for i, (src, dst) in enumerate(pairs)]
    for copy in copies:
        copy.start()
    return copies


def block_rows(start, count):
    return pl.ds(pl.multiple_of(start, LANES), count)


def held_masks(experts):
    odd = list(range(1, experts, 2))
    odd[-2:] = odd[:-3:-1]
    return [((experts - 2 * k) % experts, mask) for k, mask in enumerate(odd)]


def gather_keys(keys, experts, chips):
    axes = ("chip", "core", "expert")
    blocks = []
    for masks in held_masks(experts):
        pairs = [
            (((chip * 2 + core) * experts + e), ((chip * 2 + core) * experts + (e ^ mask)))
            for chip in range(chips)
            for core, mask in enumerate(masks)
            for e in range(experts)
        ]
        blocks.append(lax.ppermute(keys, axes, pairs))
    return blocks


def stack_kernel(*refs):
    for k, block in enumerate(refs[:-1]):
        refs[-1][k] = block[...]


def fetch_kernel(far_ref, near_ref, sem):
    copy = pltpu.make_async_copy(far_ref, near_ref, sem.at[0])
    copy.start()
    copy.wait()


def held_logits(stack_ref, tok_ref):
    blocks, rows, width = stack_ref.shape
    return lax.dot_general(
        stack_ref[...].reshape(blocks * rows, width), tok_ref[...], ROWS_BY_ROWS,
        preferred_element_type=F32,
    )


def held_logits_kernel(stack_ref, tok_ref, part_ref):
    part_ref[...] = held_logits(stack_ref, tok_ref)


def send_sums_kernel(
    swapped_ref, part_ref, tok_ref, logits_ref, weights_ref, stats_ref, send_ref, sorted_ref
):
    half = tok_ref.shape[1] // 2
    _, other = column_halves(half)
    experts, rows, count = sorted_ref.shape
    expert, core = lax.axis_index("expert"), lax.axis_index("core")
    theirs = held_logits(swapped_ref, tok_ref)
    for k, (even, odd) in enumerate(held_masks(experts)):
        held = slice(k * rows, (k + 1) * rows)
        sorted_ref[expert ^ jnp.where(core == 0, even, odd)] = part_ref[held, :]
        sorted_ref[expert ^ jnp.where(core == 0, odd, even)] = theirs[held, :]
    logits = sorted_ref[...].reshape(experts * rows, count)
    logits_ref[...] = logits
    top = jnp.max(logits, axis=1, keepdims=True)
    weights = jnp.exp(logits - top).astype(BF16)
    weights_ref[...] = weights
    total = jnp.sum(weights.astype(F32), axis=1, keepdims=True)
    send_ref[:, :half] = jnp.dot(weights, tok_ref[:, other], preferred_element_type=F32).astype(BF16)
    send_ref[:, half:] = stats_tile(top, total).astype(BF16)
    lane = lax.broadcasted_iota(jnp.int32, stats_ref.shape, 1)
    stats_ref[...] = jnp.where(lane == 0, top, total)


def keep_sums_kernel(logits_ref, weights_ref, tok_ref, keep_ref, mix_ref):
    own, _ = column_halves(keep_ref.shape[1])
    keep_ref[...] = jnp.dot(weights_ref[...], tok_ref[:, own], preferred_element_type=F32)
    logits = logits_ref[...]
    raised = jnp.exp(logits - jnp.max(logits, axis=0, keepdims=True))
    mix_ref[...] = (raised / jnp.sum(raised, axis=0, keepdims=True)).astype(BF16)


def chip_sum_kernel(keep_ref, stats_ref, came_ref, out_ref):
    half = keep_ref.shape[1]
    peers, rows, _ = out_ref.shape
    experts = keep_ref.shape[0] // rows
    top, total = stats_ref[:, 0:1], stats_ref[:, 1:2]
    came_top, came_total = read_stats(came_ref[:, half:].astype(F32))
    new_top = jnp.maximum(top, came_top)
    scale, came_scale = jnp.exp(top - new_top), jnp.exp(came_top - new_top)
    sums = (keep_ref[...] * scale + came_ref[:, :half].astype(F32) * came_scale).astype(BF16)
    tile = stats_tile(new_top, total * scale + came_total * came_scale).astype(BF16)
    sums = sums.reshape(experts, rows, half)
    tile = tile.reshape(experts, rows, LANES)
    for place, (e, _) in enumerate(peer_order(experts, peers // experts)):
        out_ref[place, :, :half] = sums[e]
        out_ref[place, :, half:] = tile[e]


def slot_inputs_of(ref):
    peers, rows, width = ref.shape
    half = width - LANES
    seqs = lax.axis_size("expert")
    blocks = [
        jnp.concatenate([ref[place] for place in places], axis=0).astype(F32)
        for places in by_chip(seqs, peers // seqs)
    ]
    stats = [read_stats(block[:, half:]) for block in blocks]
    top = functools.reduce(jnp.maximum, [s[0] for s in stats])
    scales = [jnp.exp(s[0] - top) for s in stats]
    total = sum(scale * s[1] for scale, s in zip(scales, stats))
    summed = sum(block[:, :half] * scale for block, scale in zip(blocks, scales))
    return (summed / total).astype(BF16)


def own_hidden_kernel(mine_ref, w_in_ref, acc_ref):
    own, _ = row_halves(w_in_ref)
    acc_ref[...] = jnp.dot(slot_inputs_of(mine_ref), w_in_ref[own, :], preferred_element_type=F32)


def send_terms_kernel(acc_ref, swapped_ref, w_in_ref, w_out_ref, send_ref, hidden_ref):
    _, other = row_halves(w_in_ref)
    summed = acc_ref[...] + jnp.dot(
        slot_inputs_of(swapped_ref), w_in_ref[other, :], preferred_element_type=F32
    )
    hidden = jax.nn.gelu(summed, approximate=True).astype(BF16)
    hidden_ref[...] = hidden
    _, other = column_halves(send_ref.shape[1])
    send_ref[...] = jnp.dot(hidden, w_out_ref[:, other], preferred_element_type=F32).astype(BF16)


def keep_terms_kernel(hidden_ref, w_out_ref, keep_ref):
    own, _ = column_halves(keep_ref.shape[1])
    keep_ref[...] = jnp.dot(hidden_ref[...], w_out_ref[:, own], preferred_element_type=F32)


def pair_sum_kernel(keep_ref, came_ref, out_ref):
    peers, rows, half = out_ref.shape
    seqs = keep_ref.shape[0] // rows
    sums = (keep_ref[...] + came_ref[...].astype(F32)).astype(BF16).reshape(seqs, rows, half)
    for place, (e, _) in enumerate(peer_order(seqs, peers // seqs)):
        out_ref[place] = sums[e]


def mixed_half(mix_ref, ref):
    experts = lax.axis_size("expert")
    summed = sum(
        jnp.concatenate([ref[place] for place in places], axis=0).astype(F32)
        for places in by_chip(experts, ref.shape[0] // experts)
    )
    return lax.dot_general(
        mix_ref[...], summed.astype(BF16), (((0,), (0,)), ((), ())), preferred_element_type=F32
    ).astype(BF16)


def own_mix_kernel(mix_ref, mine_ref, half_ref):
    half_ref[...] = mixed_half(mix_ref, mine_ref)


def mix_kernel(mix_ref, swapped_ref, half_ref, out_ref, rest, sem):
    own, other = column_halves(half_ref.shape[1])
    copies = copy_parts(sem, [(half_ref, out_ref.at[:, own])])
    rest[...] = mixed_half(mix_ref, swapped_ref)
    last = pltpu.make_async_copy(rest, out_ref.at[:, other], sem.at[1])
    last.start()
    copies[0].wait()
    last.wait()


def call(kernel, outs, *args, scratch=(), copies=0, in_hbm=(), stay=(), flops=0, limit=8 << 20):
    if copies:
        scratch = tuple(scratch) + (pltpu.SemaphoreType.DMA((copies,)),)
    shapes, out_specs = [], []
    for i, (shape, dtype) in enumerate(outs):
        shapes.append((pltpu.VMEM if i in stay else jax.ShapeDtypeStruct)(shape, dtype))
        out_specs.append(pl.BlockSpec(memory_space=pltpu.VMEM))
    return pl.pallas_call(
        kernel,
        out_shape=shapes,
        in_specs=[
            pl.BlockSpec(memory_space=pltpu.HBM if i in in_hbm else pltpu.VMEM)
            for i in range(len(args))
        ],
        out_specs=out_specs,
        scratch_shapes=list(scratch),
        compiler_params=pltpu.CompilerParams(vmem_limit_bytes=limit),
        cost_estimate=pl.CostEstimate(
            flops=flops,
            bytes_accessed=sum(math.prod(shape) * jnp.dtype(dtype).itemsize for shape, dtype in outs),
            transcendentals=0,
        ),
    )(*[
        pltpu.with_memory_space_constraint(a, pltpu.HBM) if i in in_hbm else a
        for i, a in enumerate(args)
    ])


def on_device(tokens, slot_keys, w_in, w_out):
    token_rows, w_in, w_out = tokens[0], w_in[0], w_out[0]
    count, width = token_rows.shape
    half = width // 2
    per_expert = slot_keys.shape[1]
    experts, chips = lax.axis_size("expert"), lax.axis_size("chip")
    slots = experts * per_expert
    units = w_in.shape[1]

    keys = slot_keys.T
    blocks = gather_keys(keys, experts, chips)
    (token_rows,) = call(
        fetch_kernel, [(token_rows.shape, BF16)], token_rows, copies=1, in_hbm=(0,), stay=(0,)
    )
    *blocks, token_rows = lax.optimization_barrier((*blocks, token_rows))
    (stack,) = call(
        stack_kernel, [((experts // 2, per_expert, width), BF16)], *blocks
    )
    swapped = lax.ppermute(stack, "core", SWAP)
    (part,) = call(
        held_logits_kernel, [((slots // 2, count), F32)], stack, token_rows,
        flops=2 * slots * count * half,
    )
    logits, weights, stats, send = call(
        send_sums_kernel,
        [
            ((slots, count), F32),
            ((slots, count), BF16),
            ((slots, LANES), F32),
            ((slots, half + LANES), BF16),
        ],
        swapped, part, token_rows,
        scratch=[pltpu.VMEM((experts, per_expert, count), F32)],
        flops=4 * slots * count * half,
    )
    came = lax.ppermute(send, "core", SWAP)
    keep, mix = call(
        keep_sums_kernel,
        [((slots, half), F32), ((slots, count), BF16)],
        logits, weights, token_rows,
        flops=2 * slots * count * half,
    )
    (packed,) = call(
        chip_sum_kernel,
        [((experts * chips, per_expert, half + LANES), BF16)],
        keep, stats, came,
        flops=COVER_FLOPS, limit=16 << 20,
    )
    groups = [
        [
            (chip * 2 + (side + 2 * e // experts) % 2) * experts + e
            for e, chip in peer_order(experts, chips)
        ]
        for side in range(2)
    ]
    exchange = functools.partial(
        lax.all_to_all, axis_name=("chip", "core", "expert"), split_axis=0, concat_axis=0,
        axis_index_groups=groups, tiled=True,
    )
    mine = exchange(packed)
    swapped = lax.ppermute(mine, "core", SWAP)
    (acc,) = call(
        own_hidden_kernel,
        [((slots, units), F32)],
        mine, w_in,
        flops=2 * slots * half * units, limit=16 << 20,
    )
    send, hidden = call(
        send_terms_kernel,
        [((slots, half), BF16), ((slots, units), BF16)],
        acc, swapped, w_in, w_out,
        flops=4 * slots * half * units, limit=16 << 20,
    )
    came = lax.ppermute(send, "core", SWAP)
    (keep,) = call(
        keep_terms_kernel, [((slots, half), F32)], hidden, w_out, flops=2 * slots * half * units
    )
    (packed,) = call(
        pair_sum_kernel, [((experts * chips, per_expert, half), BF16)], keep, came, limit=16 << 20
    )
    mine = exchange(packed)
    swapped = lax.ppermute(mine, "core", SWAP)
    (own_half,) = call(
        own_mix_kernel,
        [((count, half), BF16)],
        mix, mine,
        stay=(0,), flops=2 * slots * count * half, limit=16 << 20,
    )
    mixed = pl.pallas_call(
        mix_kernel,
        out_shape=jax.ShapeDtypeStruct((count, width), BF16),
        in_specs=[pl.BlockSpec(memory_space=pltpu.VMEM)] * 3,
        out_specs=pl.BlockSpec(memory_space=pltpu.HBM),
        scratch_shapes=[pltpu.VMEM((count, half), BF16), pltpu.SemaphoreType.DMA((2,))],
        compiler_params=pltpu.CompilerParams(vmem_limit_bytes=16 << 20),
        cost_estimate=pl.CostEstimate(
            flops=2 * slots * count * half, bytes_accessed=2 * count * width, transcendentals=0
        ),
    )(mix, swapped, own_half)
    return mixed[None]


def solution(mesh):
    sizes, names = [], []
    for name in mesh.axis_names:
        if name == "seq":
            sizes += [mesh.shape[name] // 2, 2]
            names += ["chip", "core"]
        else:
            sizes.append(mesh.shape[name])
            names.append(name)
    split = Mesh(mesh.devices.reshape(sizes), tuple(names))
    seq = ("chip", "core")
    placed = (
        P("expert", seq, None),
        P(None, "expert"),
        P("expert", None, seq),
        P("expert", seq, None),
    )
    return jax.shard_map(
        on_device, mesh=split, in_specs=placed, out_specs=P("expert", seq, None), check_vma=False
    )
```

```python
import functools
import math
import random

import jax
import jax.numpy as jnp
from jax import lax
from jax.experimental import pallas as pl
from jax.experimental.pallas import tpu as pltpu
from jax.sharding import Mesh, PartitionSpec as P

F32 = jnp.float32
BF16 = jnp.bfloat16
LANES = 128
PEER_SEED = 19
COVER_FLOPS = 10**9
SWAP = ((0, 1), (1, 0))
ROWS_BY_ROWS = (((1,), (1,)), ((), ()))


def column_halves(half):
    high = lax.axis_index("expert") // (lax.axis_size("expert") // 2)
    side = (lax.axis_index("core") + high) % 2
    own = pl.ds(pl.multiple_of(side * half, LANES), half)
    other = pl.ds(pl.multiple_of((1 - side) * half, LANES), half)
    return own, other


def row_halves(ref):
    return column_halves(ref.shape[0] // 2)


def peer_order(experts, chips):
    order = [(e, chip) for e in range(experts) for chip in range(chips)]
    random.Random(PEER_SEED).shuffle(order)
    return order


def by_chip(experts, chips):
    places = {peer: place for place, peer in enumerate(peer_order(experts, chips))}
    return [[places[e, chip] for e in range(experts)] for chip in range(chips)]


def three_terms(value):
    first = value.astype(BF16).astype(F32)
    rest = value - first
    second = rest.astype(BF16).astype(F32)
    return first, second, rest - second


def stats_tile(top, total):
    shape = top.shape[:-1] + (LANES,)
    lane = lax.broadcasted_iota(jnp.int32, shape, len(shape) - 1)
    tile = jnp.zeros(shape, F32)
    for place, term in enumerate(three_terms(top) + three_terms(total)):
        tile = jnp.where(lane == place, term, tile)
    return tile


def read_stats(tile):
    top = tile[..., 0:1] + tile[..., 1:2] + tile[..., 2:3]
    total = tile[..., 3:4] + tile[..., 4:5] + tile[..., 5:6]
    return top, total


def copy_parts(sem, pairs):
    copies = [pltpu.make_async_copy(src, dst, sem.at[i]) for i, (src, dst) in enumerate(pairs)]
    for copy in copies:
        copy.start()
    return copies


def block_rows(start, count):
    return pl.ds(pl.multiple_of(start, LANES), count)


def held_masks(experts):
    odd = list(range(1, experts, 2))
    odd[-2:] = odd[:-3:-1]
    return [((experts - 2 * k) % experts, mask) for k, mask in enumerate(odd)]


def gather_keys(keys, experts, chips):
    axes = ("chip", "core", "expert")
    blocks = []
    for masks in held_masks(experts):
        pairs = [
            (((chip * 2 + core) * experts + e), ((chip * 2 + core) * experts + (e ^ mask)))
            for chip in range(chips)
            for core, mask in enumerate(masks)
            for e in range(experts)
        ]
        blocks.append(lax.ppermute(keys, axes, pairs))
    return blocks


def stack_kernel(*refs):
    for k, block in enumerate(refs[:-1]):
        refs[-1][k] = block[...]


def fetch_kernel(far_ref, near_ref, sem):
    copy = pltpu.make_async_copy(far_ref, near_ref, sem.at[0])
    copy.start()
    copy.wait()


def held_logits(stack_ref, tok_ref):
    blocks, rows, width = stack_ref.shape
    return lax.dot_general(
        stack_ref[...].reshape(blocks * rows, width), tok_ref[...], ROWS_BY_ROWS,
        preferred_element_type=F32,
    )


def held_logits_kernel(stack_ref, tok_ref, part_ref):
    part_ref[...] = held_logits(stack_ref, tok_ref)


def send_sums_kernel(
    swapped_ref, part_ref, tok_ref, logits_ref, weights_ref, stats_ref, send_ref, sorted_ref
):
    half = tok_ref.shape[1] // 2
    _, other = column_halves(half)
    experts, rows, count = sorted_ref.shape
    expert, core = lax.axis_index("expert"), lax.axis_index("core")
    theirs = held_logits(swapped_ref, tok_ref)
    for k, (even, odd) in enumerate(held_masks(experts)):
        held = slice(k * rows, (k + 1) * rows)
        sorted_ref[expert ^ jnp.where(core == 0, even, odd)] = part_ref[held, :]
        sorted_ref[expert ^ jnp.where(core == 0, odd, even)] = theirs[held, :]
    logits = sorted_ref[...].reshape(experts * rows, count)
    logits_ref[...] = logits
    top = jnp.max(logits, axis=1, keepdims=True)
    weights = jnp.exp(logits - top).astype(BF16)
    weights_ref[...] = weights
    total = jnp.sum(weights.astype(F32), axis=1, keepdims=True)
    send_ref[:, :half] = jnp.dot(weights, tok_ref[:, other], preferred_element_type=F32).astype(BF16)
    send_ref[:, half:] = stats_tile(top, total).astype(BF16)
    lane = lax.broadcasted_iota(jnp.int32, stats_ref.shape, 1)
    stats_ref[...] = jnp.where(lane == 0, top, total)


def keep_sums_kernel(logits_ref, weights_ref, tok_ref, keep_ref, mix_ref):
    own, _ = column_halves(keep_ref.shape[1])
    keep_ref[...] = jnp.dot(weights_ref[...], tok_ref[:, own], preferred_element_type=F32)
    logits = logits_ref[...]
    raised = jnp.exp(logits - jnp.max(logits, axis=0, keepdims=True))
    mix_ref[...] = (raised / jnp.sum(raised, axis=0, keepdims=True)).astype(BF16)


def chip_sum_kernel(keep_ref, stats_ref, came_ref, out_ref):
    half = keep_ref.shape[1]
    peers, rows, _ = out_ref.shape
    experts = keep_ref.shape[0] // rows
    top, total = stats_ref[:, 0:1], stats_ref[:, 1:2]
    came_top, came_total = read_stats(came_ref[:, half:].astype(F32))
    new_top = jnp.maximum(top, came_top)
    scale, came_scale = jnp.exp(top - new_top), jnp.exp(came_top - new_top)
    sums = (keep_ref[...] * scale + came_ref[:, :half].astype(F32) * came_scale).astype(BF16)
    tile = stats_tile(new_top, total * scale + came_total * came_scale).astype(BF16)
    sums = sums.reshape(experts, rows, half)
    tile = tile.reshape(experts, rows, LANES)
    for place, (e, _) in enumerate(peer_order(experts, peers // experts)):
        out_ref[place, :, :half] = sums[e]
        out_ref[place, :, half:] = tile[e]


def slot_inputs_of(ref):
    peers, rows, width = ref.shape
    half = width - LANES
    seqs = lax.axis_size("expert")
    blocks = [
        jnp.concatenate([ref[place] for place in places], axis=0).astype(F32)
        for places in by_chip(seqs, peers // seqs)
    ]
    stats = [read_stats(block[:, half:]) for block in blocks]
    top = functools.reduce(jnp.maximum, [s[0] for s in stats])
    scales = [jnp.exp(s[0] - top) for s in stats]
    total = sum(scale * s[1] for scale, s in zip(scales, stats))
    summed = sum(block[:, :half] * scale for block, scale in zip(blocks, scales))
    return (summed / total).astype(BF16)


def own_hidden_kernel(mine_ref, w_in_ref, acc_ref):
    own, _ = row_halves(w_in_ref)
    acc_ref[...] = jnp.dot(slot_inputs_of(mine_ref), w_in_ref[own, :], preferred_element_type=F32)


def send_terms_kernel(acc_ref, swapped_ref, w_in_ref, w_out_ref, send_ref, hidden_ref):
    _, other = row_halves(w_in_ref)
    summed = acc_ref[...] + jnp.dot(
        slot_inputs_of(swapped_ref), w_in_ref[other, :], preferred_element_type=F32
    )
    hidden = jax.nn.gelu(summed, approximate=True).astype(BF16)
    hidden_ref[...] = hidden
    _, other = column_halves(send_ref.shape[1])
    send_ref[...] = jnp.dot(hidden, w_out_ref[:, other], preferred_element_type=F32).astype(BF16)


def keep_terms_kernel(hidden_ref, w_out_ref, keep_ref):
    own, _ = column_halves(keep_ref.shape[1])
    keep_ref[...] = jnp.dot(hidden_ref[...], w_out_ref[:, own], preferred_element_type=F32)


def pair_sum_kernel(keep_ref, came_ref, out_ref):
    peers, rows, half = out_ref.shape
    seqs = keep_ref.shape[0] // rows
    sums = (keep_ref[...] + came_ref[...].astype(F32)).astype(BF16).reshape(seqs, rows, half)
    for place, (e, _) in enumerate(peer_order(seqs, peers // seqs)):
        out_ref[place] = sums[e]


def mixed_half(mix_ref, ref, cols=slice(None)):
    experts = lax.axis_size("expert")
    summed = sum(
        jnp.concatenate([ref[place, :, cols] for place in places], axis=0).astype(F32)
        for places in by_chip(experts, ref.shape[0] // experts)
    )
    return lax.dot_general(
        mix_ref[...], summed.astype(BF16), (((0,), (0,)), ((), ())), preferred_element_type=F32
    ).astype(BF16)


def own_mix_kernel(mix_ref, mine_ref, half_ref):
    half_ref[...] = mixed_half(mix_ref, mine_ref)


def mix_kernel(mix_ref, swapped_ref, half_ref, out_ref, rest, sem):
    half = half_ref.shape[1]
    own, other = column_halves(half)
    copies = copy_parts(sem, [(half_ref, out_ref.at[:, own])])
    step = half // 2
    for i in range(2):
        cols = slice(i * step, (i + 1) * step)
        rest[:, cols] = mixed_half(mix_ref, swapped_ref, cols)
        place = pl.ds(pl.multiple_of(other.start + i * step, LANES), step)
        copies.append(pltpu.make_async_copy(rest.at[:, cols], out_ref.at[:, place], sem.at[1 + i]))
        copies[-1].start()
    for copy in copies:
        copy.wait()


def call(kernel, outs, *args, scratch=(), copies=0, in_hbm=(), stay=(), flops=0, limit=8 << 20):
    if copies:
        scratch = tuple(scratch) + (pltpu.SemaphoreType.DMA((copies,)),)
    shapes, out_specs = [], []
    for i, (shape, dtype) in enumerate(outs):
        shapes.append((pltpu.VMEM if i in stay else jax.ShapeDtypeStruct)(shape, dtype))
        out_specs.append(pl.BlockSpec(memory_space=pltpu.VMEM))
    return pl.pallas_call(
        kernel,
        out_shape=shapes,
        in_specs=[
            pl.BlockSpec(memory_space=pltpu.HBM if i in in_hbm else pltpu.VMEM)
            for i in range(len(args))
        ],
        out_specs=out_specs,
        scratch_shapes=list(scratch),
        compiler_params=pltpu.CompilerParams(vmem_limit_bytes=limit),
        cost_estimate=pl.CostEstimate(
            flops=flops,
            bytes_accessed=sum(math.prod(shape) * jnp.dtype(dtype).itemsize for shape, dtype in outs),
            transcendentals=0,
        ),
    )(*[
        pltpu.with_memory_space_constraint(a, pltpu.HBM) if i in in_hbm else a
        for i, a in enumerate(args)
    ])


def on_device(tokens, slot_keys, w_in, w_out):
    token_rows, w_in, w_out = tokens[0], w_in[0], w_out[0]
    count, width = token_rows.shape
    half = width // 2
    per_expert = slot_keys.shape[1]
    experts, chips = lax.axis_size("expert"), lax.axis_size("chip")
    slots = experts * per_expert
    units = w_in.shape[1]

    keys = slot_keys.T
    blocks = gather_keys(keys, experts, chips)
    (token_rows,) = call(
        fetch_kernel, [(token_rows.shape, BF16)], token_rows, copies=1, in_hbm=(0,), stay=(0,)
    )
    *blocks, token_rows = lax.optimization_barrier((*blocks, token_rows))
    (stack,) = call(
        stack_kernel, [((experts // 2, per_expert, width), BF16)], *blocks
    )
    swapped = lax.ppermute(stack, "core", SWAP)
    (part,) = call(
        held_logits_kernel, [((slots // 2, count), F32)], stack, token_rows,
        flops=2 * slots * count * half,
    )
    logits, weights, stats, send = call(
        send_sums_kernel,
        [
            ((slots, count), F32),
            ((slots, count), BF16),
            ((slots, LANES), F32),
            ((slots, half + LANES), BF16),
        ],
        swapped, part, token_rows,
        scratch=[pltpu.VMEM((experts, per_expert, count), F32)],
        flops=4 * slots * count * half,
    )
    came = lax.ppermute(send, "core", SWAP)
    keep, mix = call(
        keep_sums_kernel,
        [((slots, half), F32), ((slots, count), BF16)],
        logits, weights, token_rows,
        flops=2 * slots * count * half,
    )
    (packed,) = call(
        chip_sum_kernel,
        [((experts * chips, per_expert, half + LANES), BF16)],
        keep, stats, came,
        flops=COVER_FLOPS, limit=16 << 20,
    )
    groups = [
        [
            (chip * 2 + (side + 2 * e // experts) % 2) * experts + e
            for e, chip in peer_order(experts, chips)
        ]
        for side in range(2)
    ]
    exchange = functools.partial(
        lax.all_to_all, axis_name=("chip", "core", "expert"), split_axis=0, concat_axis=0,
        axis_index_groups=groups, tiled=True,
    )
    mine = exchange(packed)
    swapped = lax.ppermute(mine, "core", SWAP)
    (acc,) = call(
        own_hidden_kernel,
        [((slots, units), F32)],
        mine, w_in,
        flops=2 * slots * half * units, limit=16 << 20,
    )
    send, hidden = call(
        send_terms_kernel,
        [((slots, half), BF16), ((slots, units), BF16)],
        acc, swapped, w_in, w_out,
        flops=4 * slots * half * units, limit=16 << 20,
    )
    came = lax.ppermute(send, "core", SWAP)
    (keep,) = call(
        keep_terms_kernel, [((slots, half), F32)], hidden, w_out, flops=2 * slots * half * units
    )
    (packed,) = call(
        pair_sum_kernel, [((experts * chips, per_expert, half), BF16)], keep, came, limit=16 << 20
    )
    mine = exchange(packed)
    swapped = lax.ppermute(mine, "core", SWAP)
    (own_half,) = call(
        own_mix_kernel,
        [((count, half), BF16)],
        mix, mine,
        stay=(0,), flops=2 * slots * count * half, limit=16 << 20,
    )
    mixed = pl.pallas_call(
        mix_kernel,
        out_shape=jax.ShapeDtypeStruct((count, width), BF16),
        in_specs=[pl.BlockSpec(memory_space=pltpu.VMEM)] * 3,
        out_specs=pl.BlockSpec(memory_space=pltpu.HBM),
        scratch_shapes=[pltpu.VMEM((count, half), BF16), pltpu.SemaphoreType.DMA((3,))],
        compiler_params=pltpu.CompilerParams(vmem_limit_bytes=16 << 20),
        cost_estimate=pl.CostEstimate(
            flops=2 * slots * count * half, bytes_accessed=2 * count * width, transcendentals=0
        ),
    )(mix, swapped, own_half)
    return mixed[None]


def solution(mesh):
    sizes, names = [], []
    for name in mesh.axis_names:
        if name == "seq":
            sizes += [mesh.shape[name] // 2, 2]
            names += ["chip", "core"]
        else:
            sizes.append(mesh.shape[name])
            names.append(name)
    split = Mesh(mesh.devices.reshape(sizes), tuple(names))
    seq = ("chip", "core")
    placed = (
        P("expert", seq, None),
        P(None, "expert"),
        P("expert", None, seq),
        P("expert", seq, None),
    )
    return jax.shard_map(
        on_device, mesh=split, in_specs=placed, out_specs=P("expert", seq, None), check_vma=False
    )
```
